32 devices in a mesh: freq: 4 (over y, x), src: 8 (over z, core).
Axes of the slice: x: 2, y: 2, z: 4, core: 2. Of those that a mesh axis runs over, the one named last changes fastest.
Arguments:
- recorded: float32 [1024, 512, 128], P('src', 'freq'), may hold values from -0.54 to 0.54
- panels: float32 [512, 512, 128], P('src', 'freq'), may hold values from -0.18 to 0.18
Outputs:
- multiples: float32 [1024, 512, 128], P('src', 'freq')
The draws below stay inside these ranges and needn't reach their ends.
All inputs are finite; a program needn't handle non-finite values.
Results may differ from the reference program's by a relative error of at most 0.00007.
Values sent between devices are 32-bit elements; how exact they have to be, the bound alone decides.
No kernel may reach another device: no remote copies, remote signals or barrier semaphores. Data moves between devices by JAX's collectives and lax.ppermute only.
A program may use at most 128 MiB of HBM per device.

```python
import math
import jax
import jax.numpy as jnp
from jax import lax

K = 512
R = 512
NT = 128
NF = 64
SRC_DEV = 128
SOURCES = 1024


def levels(rng, extent, shards, low, largest):
    gain, own = 1.0, jax.random.fold_in(rng, 6)
    for axis_at, shards_of in shards:
        draws = jnp.exp(jax.random.uniform(jax.random.fold_in(own, axis_at), (shards_of,), jnp.float32, low / len(shards), largest / len(shards)))
        gain = gain * jnp.repeat(draws, extent[axis_at] // shards_of).reshape([-1 if axis == axis_at else 1 for axis in range(len(extent))])
    return gain


def gaussian(stream_key, extent, deviation, reach, shards=(), kind=jnp.bfloat16):
    values = deviation * jax.random.normal(stream_key, extent, jnp.float32)
    if shards:
        values = values * levels(stream_key, extent, shards, -0.22, 0.18)
    return jnp.clip(values, -reach, reach).astype(kind)


def setup_inputs(seed: int = 0) -> dict:
    streams_of = jax.random.split(jax.random.key(seed), 3)
    recorded = gaussian(streams_of[0], (SOURCES, K, NT), 0.09, 0.54, ((0, 8), (1, 4)), jnp.float32)
    panels = gaussian(streams_of[1], (K, R, NT), 0.03, 0.18, ((0, 8), (1, 4)), jnp.float32)
    return dict(recorded=recorded, panels=panels)


def lookup_tables(length, bins):
    freqs = jnp.arange(bins, dtype=jnp.int32)
    times = jnp.arange(length, dtype=jnp.int32)
    phase = (freqs[:, None] * times[None, :]) % length
    angle = (2.0 * math.pi / length) * phase.astype(jnp.float32)
    forward = jnp.stack([jnp.cos(angle), -jnp.sin(angle)], axis=1)
    weight = jnp.where(freqs == 0, 1.0, 2.0).astype(jnp.float32) / length
    inverse_transform = forward * weight[:, None, None]
    return forward, inverse_transform


def spectra(block, forward):
    return jnp.einsum('fct,abt->fcab', forward, block, precision=lax.Precision.HIGHEST)


def complex_product(left_operand, right_operand):
    upper_value = lax.Precision.HIGHEST
    real_part = jnp.einsum('vlx,vxp->vlp', left_operand[:, 0], right_operand[:, 0], precision=upper_value) - jnp.einsum('vlx,vxp->vlp', left_operand[:, 1], right_operand[:, 1], precision=upper_value)
    imaginary_part = jnp.einsum('vlx,vxp->vlp', left_operand[:, 0], right_operand[:, 1], precision=upper_value) + jnp.einsum('vlx,vxp->vlp', left_operand[:, 1], right_operand[:, 0], precision=upper_value)
    return jnp.stack([real_part, imaginary_part], axis=1)


def reference(recorded, panels):
    forward, inverse_transform = lookup_tables(NT, NF)
    panel_hat = spectra(panels, forward)
    blocks = recorded.reshape(SOURCES // SRC_DEV, SRC_DEV, K, NT)

    def one_block(block):
        predicted = complex_product(spectra(block, forward), panel_hat)
        return jnp.einsum('fcsr,fct->srt', predicted, inverse_transform, precision=lax.Precision.HIGHEST)

    result = lax.map(one_block, blocks)
    return result.reshape(SOURCES, R, NT)
```

```python
import functools

import jax
import jax.numpy as jnp
import ml_dtypes
import numpy as np
from jax import lax
from jax.experimental import pallas as pl
from jax.experimental.pallas import tpu as pltpu
from jax.sharding import PartitionSpec as P

NT = 128
NF = 64
LAST = 4
F32, BF16 = jnp.float32, jnp.bfloat16


def tables():
    phase = np.arange(NF)[:, None] * np.arange(NT)[None, :] % NT
    angle = 2.0 * np.pi / NT * phase
    forward = np.stack([np.cos(angle), -np.sin(angle)], axis=1)
    weight = np.where(np.arange(NF) == 0, 1.0, 2.0) / NT
    return forward, forward * weight[:, None, None]


def by_core(table):
    half = NF // 2
    low, high = table[:half].reshape(NF, NT), table[half:].reshape(NF, NT)
    return np.stack([np.concatenate([low, high]), np.concatenate([high, low])])


def parts(table):
    high = table.astype(ml_dtypes.bfloat16)
    low = (table - high.astype(np.float64)).astype(ml_dtypes.bfloat16)
    return high, low


def split(x):
    high = x.astype(BF16)
    return high, (x - high.astype(F32)).astype(BF16)


def bins_of(half):
    return (half - LAST, LAST)


def forward_kernel(bins, core_ref, w_ref, x_ref, *out_refs):
    rows, m, t = x_ref.shape
    high, low = split(x_ref[...].reshape(rows * m, t))
    x = jnp.concatenate([high, low], axis=1)
    both = lax.dot_general(w_ref[0], x, (((1,), (1,)), ((), ())), preferred_element_type=F32)
    n = both.shape[0] // 2
    res = both[:n] + both[n:]
    at = 0
    for out, count in zip(out_refs, bins + bins):
        for i in range(rows):
            out[:, i, :] = res[at : at + 2 * count, i * m : (i + 1) * m]
        at += 2 * count


def forward(x, core, bins):
    n, m, t = x.shape
    table = by_core(tables()[0])
    shapes = [jax.ShapeDtypeStruct((2 * b, n, m), F32) for b in bins + bins]
    high, low = parts(table)
    w = np.concatenate(
        [np.concatenate([high, high], axis=2), np.concatenate([low, np.zeros_like(low)], axis=2)], axis=1
    )
    step = 8
    return pl.pallas_call(
        functools.partial(forward_kernel, bins),
        grid_spec=pltpu.PrefetchScalarGridSpec(
            num_scalar_prefetch=1,
            grid=(n // step,),
            in_specs=[
                pl.BlockSpec((1,) + w.shape[1:], lambda i, c: (c[0], 0, 0)),
                pl.BlockSpec((step, m, t), lambda i, c: (i, 0, 0)),
            ],
            out_specs=[pl.BlockSpec((s.shape[0], step, m), lambda i, c: (0, i, 0)) for s in shapes],
        ),
        out_shape=shapes,
        cost_estimate=pl.CostEstimate(flops=12 * x.size * NT, bytes_accessed=8 * x.size, transcendentals=0),
        name="forward",
    )(core, jnp.asarray(w), x)


def product_kernel(blocks, slot_ref, *refs):
    d_refs, g_refs = refs[: 2 * blocks], refs[2 * blocks : 2 * blocks + 4 * blocks - 2]
    out_a, out_b, lhs, rhs, held = refs[6 * blocks - 2 :]
    count = d_refs[0].shape[0] // 2
    rows, depth = d_refs[0].shape[1:]
    half, cols = g_refs[0].shape[1:]
    core = slot_ref[blocks]
    base_low = 2 * depth * blocks

    def one_bin(b, carry):
        for s in range(blocks):
            slot = slot_ref[s]
            for h in range(2):
                place = jnp.where(core == h, 0, half)
                for part in range(2):
                    if s == 0:
                        g = g_refs[h][2 * b + part]
                    else:
                        up = g_refs[2 + 4 * (s - 1) + h]
                        down = g_refs[2 + 4 * (blocks - s - 1) + 2 + h]
                        g = up[2 * b + part] + down[2 * b + part]
                    high, low = split(g)
                    at = pl.multiple_of(slot * 2 * depth + place, half)
                    to = slice(part * cols, (part + 1) * cols)
                    rhs[pl.ds(at, half), to] = high
                    rhs[pl.ds(at + depth, half), to] = high
                    rhs[pl.ds(pl.multiple_of(base_low + slot * depth + place, half), half), to] = low
        for a in range(blocks):
            for h in range(2):
                for part in range(2):
                    high, low = split(d_refs[2 * a + h][2 * b + part])
                    to = slice((2 * part + h) * rows, (2 * part + h + 1) * rows)
                    lhs[to, 2 * a * depth : (2 * a + 1) * depth] = high
                    lhs[to, (2 * a + 1) * depth : (2 * a + 2) * depth] = low
                    lhs[to, base_low + a * depth : base_low + (a + 1) * depth] = high
        p = jnp.dot(lhs[...], rhs[...], preferred_element_type=F32)
        held[2 * b] = p[: 2 * rows, :cols] - p[2 * rows :, cols:]
        held[2 * b + 1] = p[: 2 * rows, cols:] + p[2 * rows :, :cols]
        return carry

    lax.fori_loop(0, count, one_bin, 0)
    for c in range(2 * count):
        out_a[:, c, :] = held[c, :rows]
        out_b[:, c, :] = held[c, rows:]


def product(slots, d, g):
    blocks = len(d) // 2
    n, rows, depth = d[0].shape
    half, cols = g[0].shape[1:]
    step = 8
    out = jax.ShapeDtypeStruct((rows, n, cols), F32)
    spec = lambda s: pl.BlockSpec((step,) + s[1:], lambda i, c: (i, 0, 0))
    return pl.pallas_call(
        functools.partial(product_kernel, blocks),
        grid_spec=pltpu.PrefetchScalarGridSpec(
            num_scalar_prefetch=1,
            grid=(n // step,),
            in_specs=[spec(x.shape) for x in list(d) + list(g)],
            out_specs=[pl.BlockSpec((rows, step, cols), lambda i, c: (0, i, 0))] * 2,
            scratch_shapes=[
                pltpu.VMEM((4 * rows, 3 * blocks * depth), BF16),
                pltpu.VMEM((3 * blocks * depth, 2 * cols), BF16),
                pltpu.VMEM((step, 2 * rows, cols), F32),
            ],
        ),
        out_shape=[out, out],
        cost_estimate=pl.CostEstimate(
            flops=n // 2 * 2 * 4 * rows * 3 * blocks * depth * 2 * cols,
            bytes_accessed=4 * sum(x.size for x in list(d) + list(g)),
            transcendentals=0,
        ),
        name="product",
    )(slots, *d, *g)


def inverse_kernel(core_ref, w_ref, *refs):
    x_refs, out = refs[:-1], refs[-1]
    for i in range(out.shape[0]):
        high, low = split(jnp.concatenate([x[i] for x in x_refs], axis=0))
        x = jnp.concatenate([high, low], axis=0)
        both = lax.dot_general(x, w_ref[0], (((0,), (0,)), ((), ())), preferred_element_type=F32)
        out[i] = both[:, :NT] + both[:, NT:]


def inverse(ms, core):
    rows, _, cols = ms[0].shape
    table = by_core(tables()[1])
    high, low = parts(table)
    w = np.concatenate(
        [np.concatenate([high, low], axis=2), np.concatenate([high, np.zeros_like(low)], axis=2)], axis=1
    )
    step = 8
    return pl.pallas_call(
        inverse_kernel,
        grid_spec=pltpu.PrefetchScalarGridSpec(
            num_scalar_prefetch=1,
            grid=(rows // step,),
            in_specs=[pl.BlockSpec((1,) + w.shape[1:], lambda i, c: (c[0], 0, 0))]
            + [pl.BlockSpec((step,) + x.shape[1:], lambda i, c: (i, 0, 0)) for x in ms],
            out_specs=pl.BlockSpec((step, cols, NT), lambda i, c: (i, 0, 0)),
        ),
        out_shape=jax.ShapeDtypeStruct((rows, cols, NT), F32),
        cost_estimate=pl.CostEstimate(
            flops=12 * rows * cols * NT * NT, bytes_accessed=8 * rows * cols * NT, transcendentals=0
        ),
        name="inverse",
    )(core, jnp.asarray(w), *ms)


def plain(recorded, panels):
    forth, back = (jnp.asarray(x, F32) for x in tables())
    best = lax.Precision.HIGHEST
    to_bins = lambda x: lax.all_to_all(
        jnp.einsum("fct,abt->fcab", forth, x, precision=best), "freq", split_axis=0, concat_axis=3, tiled=True
    )
    d = to_bins(recorded)
    g = lax.all_gather(to_bins(panels), "src", axis=2, tiled=True)
    mul = functools.partial(jnp.einsum, "fik,fkr->fir", precision=best)
    re = mul(d[:, 0], g[:, 0]) - mul(d[:, 1], g[:, 1])
    im = mul(d[:, 0], g[:, 1]) + mul(d[:, 1], g[:, 0])
    m = lax.all_to_all(jnp.stack([re, im], axis=1), "freq", split_axis=3, concat_axis=0, tiled=True)
    return jnp.einsum("fcir,fct->irt", m, back, precision=best)


def local(around, along, recorded, panels):
    tiled = all(x.shape[1] % 128 == 0 and x.shape[0] % 32 == 0 for x in (recorded, panels))
    if 2 * around != along or not tiled:
        return plain(recorded, panels)
    half = NF // 2
    levels = along // 2
    ring = list(range(around // 2)) + list(range(around - 1, around // 2 - 1, -1))
    clockwise = [(ring[i], ring[(i + 1) % around]) for i in range(around)]
    counter = [(b, a) for a, b in clockwise]
    upward = [(2 * z + c, 2 * z + 2 + c) for z in range(levels - 1) for c in range(2)]
    downward = [(b, a) for a, b in upward]
    partner = [(i, i ^ 1) for i in range(along)]

    me_ring, me_src = lax.axis_index("freq"), lax.axis_index("src")
    core, z = me_src % 2, me_src // 2
    at = jnp.where(me_ring < around // 2, me_ring, around // 2 + around - 1 - me_ring)
    core_at = core.astype(jnp.int32).reshape(1)
    bins = bins_of(half)
    chunks = len(bins)
    g_parts = forward(panels, core_at, bins)
    d_parts = forward(recorded, core_at, bins)
    swap = lambda x: lax.ppermute(x, "src", partner)
    ms = []
    for c in range(chunks):
        g_own = [g_parts[c], swap(g_parts[chunks + c])]
        d_own = [d_parts[c], swap(d_parts[chunks + c])]
        g = list(g_own)
        up, down = g_own, g_own
        for _ in range(levels - 1):
            up = [lax.ppermute(x, "src", upward) for x in up]
            down = [lax.ppermute(x, "src", downward) for x in down]
            g += up + down
        d = [d_own] + [None] * (around - 1)
        right, left = d_own, d_own
        for a in range(1, around // 2):
            right = [lax.ppermute(x, "freq", clockwise) for x in right]
            left = [lax.ppermute(x, "freq", counter) for x in left]
            d[a], d[around - a] = right, left
        d[around // 2] = [lax.ppermute(right[0], "freq", clockwise), lax.ppermute(left[1], "freq", counter)]
        d = [x for pair in d for x in pair]
        where = jnp.asarray(np.argsort(ring), jnp.int32)
        slots = (at - where[(z - jnp.arange(levels)) % levels]) % around
        slots = jnp.concatenate([slots.astype(jnp.int32), core_at])
        ms.append(product(slots, d, g))
    return inverse([m[0] for m in ms] + [swap(m[1]) for m in ms], core_at)


def solution(mesh):
    return jax.shard_map(
        functools.partial(local, mesh.shape["freq"], mesh.shape["src"]),
        mesh=mesh,
        in_specs=(P("src", "freq", None), P("src", "freq", None)),
        out_specs=P("src", "freq", None),
        check_vma=False,
    )
```

```python
import functools

import jax
import jax.numpy as jnp
import ml_dtypes
import numpy as np
from jax import lax
from jax.experimental import pallas as pl
from jax.experimental.pallas import tpu as pltpu
from jax.sharding import PartitionSpec as P


NT = 128
NF = 64
SHARES = (16, 12, 4)
F32, BF16 = jnp.float32, jnp.bfloat16


def tables():
    phase = np.arange(NF)[:, None] * np.arange(NT)[None, :] % NT
    angle = 2.0 * np.pi / NT * phase
    forward = np.stack([np.cos(angle), -np.sin(angle)], axis=1)
    weight = np.where(np.arange(NF) == 0, 1.0, 2.0) / NT
    return forward, forward * weight[:, None, None]


def by_core(table):
    half = NF // 2
    low, high = table[:half].reshape(NF, NT), table[half:].reshape(NF, NT)
    return np.stack([np.concatenate([low, high]), np.concatenate([high, low])])


def parts(table):
    high = table.astype(ml_dtypes.bfloat16)
    low = (table - high.astype(np.float64)).astype(ml_dtypes.bfloat16)
    return high, low


def split(x):
    high = x.astype(BF16)
    return high, (x - high.astype(F32)).astype(BF16)


def bins_of(half):
    return tuple(half * share // sum(SHARES) for share in SHARES)


def forward_kernel(bins, core_ref, w_ref, x_ref, *out_refs):
    rows, m, t = x_ref.shape
    high, low = split(x_ref[...].reshape(rows * m, t))
    x = jnp.concatenate([high, low], axis=1)
    both = lax.dot_general(w_ref[0], x, (((1,), (1,)), ((), ())), preferred_element_type=F32)
    n = both.shape[0] // 2
    res = both[:n] + both[n:]
    at = 0
    for out, count in zip(out_refs, bins + bins):
        for i in range(rows):
            out[:, i, :] = res[at : at + 2 * count, i * m : (i + 1) * m]
        at += 2 * count


def forward(x, core, bins):
    n, m, t = x.shape
    table = by_core(tables()[0])
    shapes = [jax.ShapeDtypeStruct((2 * b, n, m), F32) for b in bins + bins]
    high, low = parts(table)
    w = np.concatenate(
        [np.concatenate([high, high], axis=2), np.concatenate([low, np.zeros_like(low)], axis=2)], axis=1
    )
    step = 8
    return pl.pallas_call(
        functools.partial(forward_kernel, bins),
        grid_spec=pltpu.PrefetchScalarGridSpec(
            num_scalar_prefetch=1,
            grid=(n // step,),
            in_specs=[
                pl.BlockSpec((1,) + w.shape[1:], lambda i, c: (c[0], 0, 0)),
                pl.BlockSpec((step, m, t), lambda i, c: (i, 0, 0)),
            ],
            out_specs=[pl.BlockSpec((s.shape[0], step, m), lambda i, c: (0, i, 0)) for s in shapes],
        ),
        out_shape=shapes,
        cost_estimate=pl.CostEstimate(flops=12 * x.size * NT, bytes_accessed=8 * x.size, transcendentals=0),
        name="forward",
    )(core, jnp.asarray(w), x)


def product_kernel(blocks, slot_ref, *refs):
    d_refs, g_refs = refs[: 2 * blocks], list(refs[2 * blocks : -5])
    out_a, out_b, lhs, rhs, held = refs[-5:]
    if g_refs[0].ndim == 4:
        g_refs = [ref.at[h] for ref in g_refs for h in range(2)]
    count = d_refs[0].shape[0] // 2
    rows, depth = d_refs[0].shape[1:]
    half, cols = g_refs[0].shape[1:]
    core = slot_ref[blocks]
    base_low = 2 * depth * blocks

    def one_bin(b, carry):
        for s in range(blocks):
            slot = slot_ref[s]
            for h in range(2):
                place = jnp.where(core == h, 0, half)
                for part in range(2):
                    if s == 0:
                        g = g_refs[h][2 * b + part]
                    else:
                        up = g_refs[2 + 4 * (s - 1) + h]
                        down = g_refs[2 + 4 * (blocks - s - 1) + 2 + h]
                        g = up[2 * b + part] + down[2 * b + part]
                    high, low = split(g)
                    at = pl.multiple_of(slot * 2 * depth + place, half)
                    to = slice(part * cols, (part + 1) * cols)
                    rhs[pl.ds(at, half), to] = high
                    rhs[pl.ds(at + depth, half), to] = high
                    rhs[pl.ds(pl.multiple_of(base_low + slot * depth + place, half), half), to] = low
        for a in range(blocks):
            for h in range(2):
                for part in range(2):
                    high, low = split(d_refs[2 * a + h][2 * b + part])
                    to = slice((2 * part + h) * rows, (2 * part + h + 1) * rows)
                    lhs[to, 2 * a * depth : (2 * a + 1) * depth] = high
                    lhs[to, (2 * a + 1) * depth : (2 * a + 2) * depth] = low
                    lhs[to, base_low + a * depth : base_low + (a + 1) * depth] = high
        p = jnp.dot(lhs[...], rhs[...], preferred_element_type=F32)
        held[2 * b] = p[: 2 * rows, :cols] - p[2 * rows :, cols:]
        held[2 * b + 1] = p[: 2 * rows, cols:] + p[2 * rows :, :cols]
        return carry

    lax.fori_loop(0, count, one_bin, 0)
    for c in range(2 * count):
        out_a[:, c, :] = held[c, :rows]
        out_b[:, c, :] = held[c, rows:]


def product(slots, d, g):
    blocks = len(d) // 2
    n, rows, depth = d[0].shape
    _, cols = g[0].shape[-2:]
    step = 8
    out = jax.ShapeDtypeStruct((rows, n, cols), F32)

    def spec(s):
        if len(s) == 4:
            return pl.BlockSpec((2, step) + s[2:], lambda i, c: (0, i, 0, 0))
        return pl.BlockSpec((step,) + s[1:], lambda i, c: (i, 0, 0))

    return pl.pallas_call(
        functools.partial(product_kernel, blocks),
        grid_spec=pltpu.PrefetchScalarGridSpec(
            num_scalar_prefetch=1,
            grid=(n // step,),
            in_specs=[spec(x.shape) for x in list(d) + list(g)],
            out_specs=[pl.BlockSpec((rows, step, cols), lambda i, c: (0, i, 0))] * 2,
            scratch_shapes=[
                pltpu.VMEM((4 * rows, 3 * blocks * depth), BF16),
                pltpu.VMEM((3 * blocks * depth, 2 * cols), BF16),
                pltpu.VMEM((step, 2 * rows, cols), F32),
            ],
        ),
        out_shape=[out, out],
        cost_estimate=pl.CostEstimate(
            flops=n // 2 * 2 * 4 * rows * 3 * blocks * depth * 2 * cols,
            bytes_accessed=4 * sum(x.size for x in list(d) + list(g)),
            transcendentals=0,
        ),
        name="product",
    )(slots, *d, *g)


def inverse_kernel(so_far, core_ref, w_ref, *refs):
    x_refs, out = refs[so_far:-1], refs[-1]
    for i in range(out.shape[0]):
        high, low = split(jnp.concatenate([x[i] for x in x_refs], axis=0))
        x = jnp.concatenate([high, low], axis=0)
        both = lax.dot_general(x, w_ref[0], (((0,), (0,)), ((), ())), preferred_element_type=F32)
        res = both[:, :NT] + both[:, NT:]
        out[i] = res + refs[0][i] if so_far else res


def inverse(ms, core, cuts, acc=None):
    rows, _, cols = ms[0].shape
    half = NF
    table = by_core(tables()[1])
    table = np.concatenate([table[:, a:b] for a, b in cuts] + [table[:, half + a : half + b] for a, b in cuts], axis=1)
    accs = [] if acc is None else [acc]
    high, low = parts(table)
    w = np.concatenate(
        [np.concatenate([high, low], axis=2), np.concatenate([high, np.zeros_like(low)], axis=2)], axis=1
    )
    step = 8
    return pl.pallas_call(
        functools.partial(inverse_kernel, len(accs)),
        grid_spec=pltpu.PrefetchScalarGridSpec(
            num_scalar_prefetch=1,
            grid=(rows // step,),
            in_specs=[pl.BlockSpec((1,) + w.shape[1:], lambda i, c: (c[0], 0, 0))]
            + [pl.BlockSpec((step,) + x.shape[1:], lambda i, c: (i, 0, 0)) for x in accs + ms],
            out_specs=pl.BlockSpec((step, cols, NT), lambda i, c: (i, 0, 0)),
        ),
        out_shape=jax.ShapeDtypeStruct((rows, cols, NT), F32),
        cost_estimate=pl.CostEstimate(
            flops=12 * rows * cols * NT * NT, bytes_accessed=8 * rows * cols * NT, transcendentals=0
        ),
        name="inverse",
    )(core, jnp.asarray(w), *accs, *ms)


def plain(recorded, panels):
    forth, back = (jnp.asarray(x, F32) for x in tables())
    best = lax.Precision.HIGHEST
    to_bins = lambda x: lax.all_to_all(
        jnp.einsum("fct,abt->fcab", forth, x, precision=best), "freq", split_axis=0, concat_axis=3, tiled=True
    )
    d = to_bins(recorded)
    g = lax.all_gather(to_bins(panels), "src", axis=2, tiled=True)
    mul = functools.partial(jnp.einsum, "fik,fkr->fir", precision=best)
    re = mul(d[:, 0], g[:, 0]) - mul(d[:, 1], g[:, 1])
    im = mul(d[:, 0], g[:, 1]) + mul(d[:, 1], g[:, 0])
    m = lax.all_to_all(jnp.stack([re, im], axis=1), "freq", split_axis=3, concat_axis=0, tiled=True)
    return jnp.einsum("fcir,fct->irt", m, back, precision=best)


def local(around, along, recorded, panels):
    tiled = all(x.shape[1] % 128 == 0 and x.shape[0] % 32 == 0 for x in (recorded, panels))
    if around != 4 or along != 8 or not tiled:
        return plain(recorded, panels)
    half = NF // 2
    levels = along // 2
    ring = list(range(around // 2)) + list(range(around - 1, around // 2 - 1, -1))
    clockwise = [(ring[i], ring[(i + 1) % around]) for i in range(around)]
    counter = [(b, a) for a, b in clockwise]
    upward = [(2 * z + c, 2 * z + 2 + c) for z in range(levels - 1) for c in range(2)]
    downward = [(b, a) for a, b in upward]
    partner = [(i, i ^ 1) for i in range(along)]

    me_ring, me_src = lax.axis_index("freq"), lax.axis_index("src")
    core, z = me_src % 2, me_src // 2
    at = jnp.where(me_ring < around // 2, me_ring, around // 2 + around - 1 - me_ring)
    core_at = core.astype(jnp.int32).reshape(1)
    bins = bins_of(half)
    chunks = len(bins)
    where = jnp.asarray(np.argsort(ring), jnp.int32)
    slots = (at - where[(z - jnp.arange(levels)) % levels]) % around
    slots = jnp.concatenate([slots.astype(jnp.int32), core_at])

    g_parts = forward(panels, core_at, bins)
    d_parts = forward(recorded, core_at, bins)
    ms = []
    for c in range(chunks):
        g_own = [g_parts[c], lax.ppermute(g_parts[chunks + c], "src", partner)]
        d_own = [d_parts[c], lax.ppermute(d_parts[chunks + c], "src", partner)]
        if c:
            g_own = [jnp.stack(g_own)]
        g = list(g_own)
        up, down = g_own, g_own
        for _ in range(1, levels):
            up = [lax.ppermute(x, "src", upward) for x in up]
            down = [lax.ppermute(x, "src", downward) for x in down]
            g += up + down
        d = [d_own] + [None] * (around - 1)
        right, left = d_own, d_own
        for a in range(1, around // 2):
            right = [lax.ppermute(x, "freq", clockwise) for x in right]
            left = [lax.ppermute(x, "freq", counter) for x in left]
            d[a], d[around - a] = right, left
        last = around // 2
        d[last] = [lax.ppermute(right[0], "freq", clockwise), lax.ppermute(left[1], "freq", counter)]
        d = [x for pair in d for x in pair]
        m = product(slots, d, g)
        ms.append([m[0], lax.ppermute(m[1], "src", partner)])
    edges = np.cumsum([0] + [2 * b for b in bins])
    cuts = list(zip(edges[:-1], edges[1:]))
    acc = inverse([m for pair in zip(*ms[:1]) for m in pair], core_at, cuts[:1])
    return inverse([m for pair in zip(*ms[1:]) for m in pair], core_at, cuts[1:], acc)


def solution(mesh):
    return jax.shard_map(
        functools.partial(local, mesh.shape["freq"], mesh.shape["src"]),
        mesh=mesh,
        in_specs=(P("src", "freq", None), P("src", "freq", None)),
        out_specs=P("src", "freq", None),
        check_vma=False,
    )
```

```python
import functools

import jax
import jax.numpy as jnp
import ml_dtypes
import numpy as np
from jax import lax
from jax.experimental import pallas as pl
from jax.experimental.pallas import tpu as pltpu
from jax.sharding import PartitionSpec as P


NT = 128
NF = 64
SHARES = (24, 8)
F32, BF16 = jnp.float32, jnp.bfloat16


def tables():
    phase = np.arange(NF)[:, None] * np.arange(NT)[None, :] % NT
    angle = 2.0 * np.pi / NT * phase
    forward = np.stack([np.cos(angle), -np.sin(angle)], axis=1)
    weight = np.where(np.arange(NF) == 0, 1.0, 2.0) / NT
    return forward, forward * weight[:, None, None]


def by_core(table):
    half = NF // 2
    low, high = table[:half].reshape(NF, NT), table[half:].reshape(NF, NT)
    return np.stack([np.concatenate([low, high]), np.concatenate([high, low])])


def parts(table):
    high = table.astype(ml_dtypes.bfloat16)
    low = (table - high.astype(np.float64)).astype(ml_dtypes.bfloat16)
    return high, low


def split(x):
    high = x.astype(BF16)
    return high, (x - high.astype(F32)).astype(BF16)


def bins_of(half):
    return tuple(half * share // sum(SHARES) for share in SHARES)


def forward_kernel(counts, core_ref, w_ref, x_ref, *out_refs):
    rows, m, t = x_ref.shape
    group = 8

    def some(q, carry):
        first = pl.multiple_of(q * group, group)
        high, low = split(x_ref[pl.ds(first, group)].reshape(group * m, t))
        x = jnp.concatenate([high, low], axis=1)
        both = lax.dot_general(w_ref[0], x, (((1,), (1,)), ((), ())), preferred_element_type=F32)
        n = both.shape[0] // 2
        res = both[:n] + both[n:]
        at = 0
        for out, count in zip(out_refs, counts):
            view = out.at[:, pl.ds(first, group), :]
            for i in range(group):
                view[:, i, :] = res[at : at + count, i * m : (i + 1) * m]
            at += count
        return carry

    lax.fori_loop(0, rows // group, some, 0)


def forward(x, core, cuts):
    n, m, t = x.shape
    table = by_core(tables()[0])
    table = np.concatenate([table[:, a:b] for a, b in cuts], axis=1)
    counts = [b - a for a, b in cuts]
    shapes = [jax.ShapeDtypeStruct((count, n, m), F32) for count in counts]
    high, low = parts(table)
    w = np.concatenate(
        [np.concatenate([high, high], axis=2), np.concatenate([low, np.zeros_like(low)], axis=2)], axis=1
    )
    step = 32
    return pl.pallas_call(
        functools.partial(forward_kernel, counts),
        grid_spec=pltpu.PrefetchScalarGridSpec(
            num_scalar_prefetch=1,
            grid=(n // step,),
            in_specs=[
                pl.BlockSpec((1,) + w.shape[1:], lambda i, c: (c[0], 0, 0)),
                pl.BlockSpec((step, m, t), lambda i, c: (i, 0, 0)),
            ],
            out_specs=[pl.BlockSpec((s.shape[0], step, m), lambda i, c: (0, i, 0)) for s in shapes],
        ),
        out_shape=shapes,
        cost_estimate=pl.CostEstimate(flops=12 * x.size * NT, bytes_accessed=8 * x.size, transcendentals=0),
        name="forward",
    )(core, jnp.asarray(w), x)


def product_kernel(blocks, slot_ref, *refs):
    d_refs, g_refs = refs[: 2 * blocks], list(refs[2 * blocks : -5])
    out_a, out_b, lhs, rhs, held = refs[-5:]
    if g_refs[0].ndim == 4:
        g_refs = [ref.at[h] for ref in g_refs for h in range(2)]
    count = d_refs[0].shape[0] // 2
    rows, depth = d_refs[0].shape[1:]
    half, cols = g_refs[0].shape[1:]
    core = slot_ref[blocks]
    base_low = 2 * depth * blocks
    step, steps = pl.program_id(0), pl.num_programs(0)
    for b in range(count):
        for s in range(blocks):
            slot = slot_ref[s]
            for h in range(2):
                place = jnp.where(core == h, 0, half)
                for part in range(2):
                    if s == 0:
                        g = g_refs[h][2 * b + part]
                    else:
                        up = g_refs[2 + 4 * (s - 1) + h]
                        down = g_refs[2 + 4 * (blocks - s - 1) + 2 + h]
                        g = up[2 * b + part] + down[2 * b + part]
                    high, low = split(g)
                    at = pl.multiple_of(slot * 2 * depth + place, half)
                    to = slice(part * cols, (part + 1) * cols)
                    rhs[b % 2, pl.ds(at, half), to] = high
                    rhs[b % 2, pl.ds(at + depth, half), to] = high
                    rhs[b % 2, pl.ds(pl.multiple_of(base_low + slot * depth + place, half), half), to] = low
        for a in range(blocks):
            for h in range(2):
                for part in range(2):
                    high, low = split(d_refs[2 * a + h][2 * b + part])
                    to = slice((2 * part + h) * rows, (2 * part + h + 1) * rows)
                    lhs[b % 2, to, 2 * a * depth : (2 * a + 1) * depth] = high
                    lhs[b % 2, to, (2 * a + 1) * depth : (2 * a + 2) * depth] = low
                    lhs[b % 2, to, base_low + a * depth : base_low + (a + 1) * depth] = high
        p = jnp.dot(lhs[b % 2], rhs[b % 2], preferred_element_type=F32)
        row = 2 * (step * count + b)
        held[row] = p[: 2 * rows, :cols] - p[2 * rows :, cols:]
        held[row + 1] = p[: 2 * rows, cols:] + p[2 * rows :, :cols]

    @pl.when(step == steps - 1)
    def _():
        for c in range(held.shape[0]):
            out_a[:, c, :] = held[c, :rows]
            out_b[:, c, :] = held[c, rows:]


def product(slots, d, g):
    blocks = len(d) // 2
    n, rows, depth = d[0].shape
    _, cols = g[0].shape[-2:]
    step = 4
    out = jax.ShapeDtypeStruct((rows, n, cols), F32)
    each = 1 if g[0].ndim == 4 else 2

    def spec(x, hop=None):
        def at(i, c):
            if hop is None:
                return i
            z = c[blocks + 1]
            there = z >= hop[1] if hop[0] else z + hop[1] < blocks
            return jnp.where(there, i, 0)

        if x.ndim == 4:
            return pl.BlockSpec((2, step) + x.shape[2:], lambda i, c: (0, at(i, c), 0, 0))
        return pl.BlockSpec((step,) + x.shape[1:], lambda i, c: (at(i, c), 0, 0))

    hops = [None] * each
    for s in range(1, blocks):
        hops += [(True, s)] * each + [(False, s)] * each
    return pl.pallas_call(
        functools.partial(product_kernel, blocks),
        grid_spec=pltpu.PrefetchScalarGridSpec(
            num_scalar_prefetch=1,
            grid=(n // step,),
            in_specs=[spec(x) for x in d] + [spec(x, hop) for x, hop in zip(g, hops)],
            out_specs=[pl.BlockSpec((rows, n, cols), lambda i, c: (0, 0, 0))] * 2,
            scratch_shapes=[
                pltpu.VMEM((2, 4 * rows, 3 * blocks * depth), BF16),
                pltpu.VMEM((2, 3 * blocks * depth, 2 * cols), BF16),
                pltpu.VMEM((n, 2 * rows, cols), F32),
            ],
        ),
        out_shape=[out, out],
        cost_estimate=pl.CostEstimate(
            flops=n // 2 * 2 * 4 * rows * 3 * blocks * depth * 2 * cols,
            bytes_accessed=4 * sum(x.size for x in list(d) + list(g)),
            transcendentals=0,
        ),
        name="product",
    )(slots, *d, *g)


def inverse_kernel(core_ref, w_ref, *refs):
    x_refs, out = refs[:-1], refs[-1]
    group = 8

    def some(q, carry):
        for u in range(group):
            i = q * group + u
            high, low = split(jnp.concatenate([x[i] for x in x_refs], axis=0))
            x = jnp.concatenate([high, low], axis=0)
            both = lax.dot_general(x, w_ref[0], (((0,), (0,)), ((), ())), preferred_element_type=F32)
            out[i] = both[:, :NT] + both[:, NT:]
        return carry

    lax.fori_loop(0, out.shape[0] // group, some, 0)


def inverse(ms, core):
    rows, _, cols = ms[0].shape
    high, low = parts(by_core(tables()[1]))
    w = np.concatenate(
        [np.concatenate([high, low], axis=2), np.concatenate([high, np.zeros_like(low)], axis=2)], axis=1
    )
    step = 32
    return pl.pallas_call(
        inverse_kernel,
        grid_spec=pltpu.PrefetchScalarGridSpec(
            num_scalar_prefetch=1,
            grid=(rows // step,),
            in_specs=[pl.BlockSpec((1,) + w.shape[1:], lambda i, c: (c[0], 0, 0))]
            + [pl.BlockSpec((step,) + x.shape[1:], lambda i, c: (i, 0, 0)) for x in ms],
            out_specs=pl.BlockSpec((step, cols, NT), lambda i, c: (i, 0, 0)),
        ),
        out_shape=jax.ShapeDtypeStruct((rows, cols, NT), F32),
        cost_estimate=pl.CostEstimate(
            flops=12 * rows * cols * NT * NT, bytes_accessed=8 * rows * cols * NT, transcendentals=0
        ),
        name="inverse",
    )(core, jnp.asarray(w), *ms)


def plain(recorded, panels):
    forth, back = (jnp.asarray(x, F32) for x in tables())
    best = lax.Precision.HIGHEST
    to_bins = lambda x: lax.all_to_all(
        jnp.einsum("fct,abt->fcab", forth, x, precision=best), "freq", split_axis=0, concat_axis=3, tiled=True
    )
    d = to_bins(recorded)
    g = lax.all_gather(to_bins(panels), "src", axis=2, tiled=True)
    mul = functools.partial(jnp.einsum, "fik,fkr->fir", precision=best)
    re = mul(d[:, 0], g[:, 0]) - mul(d[:, 1], g[:, 1])
    im = mul(d[:, 0], g[:, 1]) + mul(d[:, 1], g[:, 0])
    m = lax.all_to_all(jnp.stack([re, im], axis=1), "freq", split_axis=3, concat_axis=0, tiled=True)
    return jnp.einsum("fcir,fct->irt", m, back, precision=best)


def local(around, along, recorded, panels):
    tiled = all(x.shape[1] % 128 == 0 and x.shape[0] % 32 == 0 for x in (recorded, panels))
    if around != 4 or along != 8 or not tiled:
        return plain(recorded, panels)
    half = NF // 2
    levels = along // 2
    ring = list(range(around // 2)) + list(range(around - 1, around // 2 - 1, -1))
    clockwise = [(ring[i], ring[(i + 1) % around]) for i in range(around)]
    counter = [(b, a) for a, b in clockwise]
    upward = [(2 * z + c, 2 * z + 2 + c) for z in range(levels - 1) for c in range(2)]
    downward = [(b, a) for a, b in upward]
    partner = [(i, i ^ 1) for i in range(along)]

    me_ring, me_src = lax.axis_index("freq"), lax.axis_index("src")
    core, z = me_src % 2, me_src // 2
    at = jnp.where(me_ring < around // 2, me_ring, around // 2 + around - 1 - me_ring)
    core_at = core.astype(jnp.int32).reshape(1)
    bins = bins_of(half)
    chunks = len(bins)
    where = jnp.asarray(np.argsort(ring), jnp.int32)
    slots = (at - where[(z - jnp.arange(levels)) % levels]) % around
    slots = jnp.concatenate([slots.astype(jnp.int32), core_at, z.astype(jnp.int32).reshape(1)])
    edges = [int(e) for e in np.cumsum([0] + [2 * b for b in bins])]
    cuts = list(zip(edges[:-1], edges[1:]))
    cuts += [(NF + a, NF + b) for a, b in cuts]

    g_parts, d_parts = [], []
    for which in (cuts[:1], cuts[1:]):
        for x, to in ((panels, g_parts), (recorded, d_parts)):
            to += forward(x, core_at, which)
    ms = []
    for c in range(chunks):
        g_own = [g_parts[c], lax.ppermute(g_parts[chunks + c], "src", partner)]
        d_own = [d_parts[c], lax.ppermute(d_parts[chunks + c], "src", partner)]
        if c:
            g_own = [jnp.stack(g_own)]
        g = list(g_own)
        up, down = g_own, g_own
        for _ in range(1, levels):
            up = [lax.ppermute(x, "src", upward) for x in up]
            down = [lax.ppermute(x, "src", downward) for x in down]
            g += up + down
        d = [d_own] + [None] * (around - 1)
        right, left = d_own, d_own
        for a in range(1, around // 2):
            right = [lax.ppermute(x, "freq", clockwise) for x in right]
            left = [lax.ppermute(x, "freq", counter) for x in left]
            d[a], d[around - a] = right, left
        last = around // 2
        d[last] = [lax.ppermute(right[0], "freq", clockwise), lax.ppermute(left[1], "freq", counter)]
        d = [x for pair in d for x in pair]
        m = product(slots, d, g)
        ms.append([m[0], lax.ppermute(m[1], "src", partner)])
    return inverse([m[0] for m in ms] + [m[1] for m in ms], core_at)


def solution(mesh):
    return jax.shard_map(
        functools.partial(local, mesh.shape["freq"], mesh.shape["src"]),
        mesh=mesh,
        in_specs=(P("src", "freq", None), P("src", "freq", None)),
        out_specs=P("src", "freq", None),
        check_vma=False,
    )
```

```python
import functools

import jax
import jax.numpy as jnp
import ml_dtypes
import numpy as np
from jax import lax
from jax.experimental import pallas as pl
from jax.experimental.pallas import tpu as pltpu
from jax.sharding import PartitionSpec as P


NT = 128
NF = 64
SHARES = (20, 12)
F32, BF16 = jnp.float32, jnp.bfloat16


def tables():
    phase = np.arange(NF)[:, None] * np.arange(NT)[None, :] % NT
    angle = 2.0 * np.pi / NT * phase
    forward = np.stack([np.cos(angle), -np.sin(angle)], axis=1)
    weight = np.where(np.arange(NF) == 0, 1.0, 2.0) / NT
    return forward, forward * weight[:, None, None]


def by_core(table):
    half = NF // 2
    low, high = table[:half].reshape(NF, NT), table[half:].reshape(NF, NT)
    return np.stack([np.concatenate([low, high]), np.concatenate([high, low])])


def parts(table):
    high = table.astype(ml_dtypes.bfloat16)
    low = (table - high.astype(np.float64)).astype(ml_dtypes.bfloat16)
    return high, low


def split(x):
    high = x.astype(BF16)
    return high, (x - high.astype(F32)).astype(BF16)


def bins_of(half):
    return tuple(half * share // sum(SHARES) for share in SHARES)


def forward_kernel(counts, core_ref, w_ref, x_ref, *out_refs):
    rows, m, t = x_ref.shape
    group = 8

    def some(q, carry):
        first = pl.multiple_of(q * group, group)
        high, low = split(x_ref[pl.ds(first, group)].reshape(group * m, t))
        x = jnp.concatenate([high, low], axis=1)
        both = lax.dot_general(w_ref[0], x, (((1,), (1,)), ((), ())), preferred_element_type=F32)
        n = both.shape[0] // 2
        res = both[:n] + both[n:]
        at = 0
        for out, count in zip(out_refs, counts):
            view = out.at[:, pl.ds(first, group), :]
            for i in range(group):
                view[:, i, :] = res[at : at + count, i * m : (i + 1) * m]
            at += count
        return carry

    lax.fori_loop(0, rows // group, some, 0)


def forward(x, core, cuts, start=0, n=None):
    m, t = x.shape[1:]
    n = x.shape[0] if n is None else n
    table = by_core(tables()[0])
    table = np.concatenate([table[:, a:b] for a, b in cuts], axis=1)
    counts = [b - a for a, b in cuts]
    shapes = [jax.ShapeDtypeStruct((count, n, m), F32) for count in counts]
    high, low = parts(table)
    w = np.concatenate(
        [np.concatenate([high, high], axis=2), np.concatenate([low, np.zeros_like(low)], axis=2)], axis=1
    )
    step = 32 if n > 64 else 16
    return pl.pallas_call(
        functools.partial(forward_kernel, counts),
        grid_spec=pltpu.PrefetchScalarGridSpec(
            num_scalar_prefetch=1,
            grid=(n // step,),
            in_specs=[
                pl.BlockSpec((1,) + w.shape[1:], lambda i, c: (c[0], 0, 0)),
                pl.BlockSpec((step, m, t), lambda i, c: (i + start // step, 0, 0)),
            ],
            out_specs=[pl.BlockSpec((s.shape[0], step, m), lambda i, c: (0, i, 0)) for s in shapes],
        ),
        out_shape=shapes,
        cost_estimate=pl.CostEstimate(
            flops=12 * n * m * t * NT, bytes_accessed=8 * n * m * t, transcendentals=0
        ),
        name="forward",
    )(core, jnp.asarray(w), x)


ALL, EARLY, LATE = range(3)


def sides(part, levels):
    pairs = [[("own", 0)]] + [[("up", s), ("down", levels - s)] for s in range(1, levels)]
    return [[x for x in pair if part != EARLY or x[1] < levels - 1] for pair in pairs]


def product_kernel(part, levels, places, d_keys, g_keys, slot_ref, *refs):
    d_refs = {}
    for (a, at), ref in zip(d_keys, refs):
        d_refs.setdefault(a, []).append((at, ref))
    g_refs = {}
    for (way, hop, h), ref in zip(g_keys, refs[len(d_keys) :]):
        for i in range(2) if h is None else (h,):
            g_refs[way, hop, i] = ref.at[i] if h is None else ref
    rest = refs[len(d_keys) + len(g_keys) :]
    lhs, rhs = rest[-2:]
    count = refs[0].shape[0] // 2
    depth = refs[0].shape[2]
    rows = lhs.shape[1] // 4
    half, cols = next(iter(g_refs.values())).shape[1:]
    core, chosen, far = (slot_ref[levels + i] for i in range(3))
    step, steps = pl.program_id(0), pl.num_programs(0)

    def put_g(b, slot, h, half_of, g):
        high, low = split(g)
        place = jnp.where(core == h, 0, half)
        at = pl.multiple_of(slot * 3 * depth + place, half)
        to = slice(half_of * cols, (half_of + 1) * cols)
        for i, value in enumerate((high, high, low)):
            rhs[b % 2, pl.ds(at + i * depth, half), to] = value

    def put_d(b, place, a):
        for at, ref in d_refs[a]:
            for half_of in range(2):
                high, low = split(ref[2 * b + half_of])
                first = 2 * rows * half_of + at
                for i, value in enumerate((high, low, high)):
                    to = slice((3 * place + i) * depth, (3 * place + i + 1) * depth)
                    lhs[b % 2, first : first + ref.shape[1], to] = value

    for b in range(count):
        for h in range(2):
            for half_of in range(2):
                row = 2 * b + half_of
                for s, pair in enumerate(sides(part, levels)):
                    put_g(b, slot_ref[s], h, half_of, sum(g_refs[way, hop, h][row] for way, hop in pair))
                if part == LATE:
                    last = g_refs["up", levels - 1, h][row] + g_refs["down", levels - 1, h][row]
                    put_g(b, 1, h, half_of, jnp.where(far > 0, last, 0.0))
        for place, which in enumerate(places):
            if len(which) == 1:
                put_d(b, place, which[0])
            else:
                for a in which:
                    pl.when(chosen == a)(functools.partial(put_d, b, place, a))
        deep = 3 * depth * len(places)
        p = jnp.dot(lhs[b % 2, :, :deep], rhs[b % 2, :deep, :], preferred_element_type=F32)
        real = p[: 2 * rows, :cols] - p[2 * rows :, cols:]
        imaginary = p[: 2 * rows, cols:] + p[2 * rows :, :cols]
        if part == EARLY:
            rest[0][2 * b], rest[0][2 * b + 1] = real, imaginary
            continue
        if part == LATE:
            real, imaginary = real + rest[0][2 * b], imaginary + rest[0][2 * b + 1]
        held = rest[-3]
        row = 2 * (step * count + b)
        held[row], held[row + 1] = real, imaginary

    if part != EARLY:

        @pl.when(step == steps - 1)
        def _():
            out_a, out_b, held = rest[-5:-2]
            for c in range(held.shape[0]):
                out_a[:, c, :] = held[c, :rows]
                out_b[:, c, :] = held[c, rows:]


def product(part, me, d, g, so_far=None):
    slot, core, z = me
    levels = slot.shape[0]
    around = len(d)
    diag = around // 2
    depth = d[0][0].shape[2]
    n = d[0][0].shape[0]
    rows = sum(x.shape[1] for x in d[0]) // 2
    _, cols = g["own", 0][0].shape[-2:]
    step = 4

    far_s = jnp.where(z == 0, 1, levels - 1)
    far_a = slot[far_s]
    far = ((z == 0) | (z == levels - 1)) & (far_a != diag)
    chosen = jnp.where(far, far_a, 0)
    others = [a for a in range(around) if a != diag]
    if part == ALL:
        places, to = [[a] for a in range(around)], slot
    elif part == EARLY:
        index = np.array([others.index(a) if a in others else len(others) for a in range(around)])
        places, to = [[a] for a in others], jnp.asarray(index)[slot]
    else:
        places, to = [[diag], others], jnp.where(slot == diag, 0, 2)
    scalars = [to, jnp.stack([core, chosen, far.astype(jnp.int32)])]

    operands, d_keys, g_keys, needed = [], [], [], []
    for a in sorted(set(sum(places, []))):
        at = 0
        for x in d[a]:
            d_keys.append((a, at))
            operands.append(x)
            needed.append(jnp.where(chosen == a, 1, 0) if part == LATE and a != diag else 1)
            at += x.shape[1]
    for s, pair in enumerate(sides(part, levels)):
        for way, hop in pair:
            there = {"own": True, "up": z >= hop, "down": z + hop < levels}[way]
            if part == LATE:
                there = there & ((slot[s] == diag) | (hop == levels - 1))
            for h, x in enumerate(g[way, hop]):
                g_keys.append((way, hop, h if len(g[way, hop]) == 2 else None))
                operands.append(x)
                needed.append(jnp.where(there, 1, 0))
    if so_far is not None:
        operands.append(so_far)
        needed.append(1)
    scalars.append(jnp.stack([jnp.asarray(x, jnp.int32) for x in needed]))
    scalars = jnp.concatenate([x.astype(jnp.int32) for x in scalars])
    first = levels + 3

    def spec(i, x):
        at = lambda j, c: jnp.where(c[first + i] > 0, j, 0)
        if x.ndim == 4:
            return pl.BlockSpec((2, step) + x.shape[2:], lambda j, c: (0, at(j, c), 0, 0))
        return pl.BlockSpec((step,) + x.shape[1:], lambda j, c: (at(j, c), 0, 0))

    scratch = [
        pltpu.VMEM((2, 4 * rows, 3 * depth * len(places)), BF16),
        pltpu.VMEM((2, 3 * depth * (len(places) + 1), 2 * cols), BF16),
    ]
    if part == EARLY:
        out = jax.ShapeDtypeStruct((n, 2 * rows, cols), F32)
        out_specs = pl.BlockSpec((step, 2 * rows, cols), lambda i, c: (i, 0, 0))
    else:
        out = [jax.ShapeDtypeStruct((rows, n, cols), F32)] * 2
        out_specs = [pl.BlockSpec((rows, n, cols), lambda i, c: (0, 0, 0))] * 2
        scratch = [pltpu.VMEM((n, 2 * rows, cols), F32)] + scratch
    return pl.pallas_call(
        functools.partial(product_kernel, part, levels, places, d_keys, g_keys),
        grid_spec=pltpu.PrefetchScalarGridSpec(
            num_scalar_prefetch=1,
            grid=(n // step,),
            in_specs=[spec(i, x) for i, x in enumerate(operands)],
            out_specs=out_specs,
            scratch_shapes=scratch,
        ),
        out_shape=out,
        cost_estimate=pl.CostEstimate(
            flops=n // 2 * 2 * 4 * rows * 3 * len(places) * depth * 2 * cols,
            bytes_accessed=4 * sum(x.size for x in operands),
            transcendentals=0,
        ),
    )(scalars, *operands)


def inverse_kernel(core_ref, w_ref, *refs):
    x_refs, out = refs[:-1], refs[-1]
    group = 8

    def some(q, carry):
        for u in range(group):
            i = q * group + u
            high, low = split(jnp.concatenate([x[i] for x in x_refs], axis=0))
            x = jnp.concatenate([high, low], axis=0)
            both = lax.dot_general(x, w_ref[0], (((0,), (0,)), ((), ())), preferred_element_type=F32)
            out[i] = both[:, :NT] + both[:, NT:]
        return carry

    lax.fori_loop(0, out.shape[0] // group, some, 0)


def inverse(ms, core):
    rows, _, cols = ms[0].shape
    high, low = parts(by_core(tables()[1]))
    w = np.concatenate(
        [np.concatenate([high, low], axis=2), np.concatenate([high, np.zeros_like(low)], axis=2)], axis=1
    )
    step = 32
    return pl.pallas_call(
        inverse_kernel,
        grid_spec=pltpu.PrefetchScalarGridSpec(
            num_scalar_prefetch=1,
            grid=(rows // step,),
            in_specs=[pl.BlockSpec((1,) + w.shape[1:], lambda i, c: (c[0], 0, 0))]
            + [pl.BlockSpec((step,) + x.shape[1:], lambda i, c: (i, 0, 0)) for x in ms],
            out_specs=pl.BlockSpec((step, cols, NT), lambda i, c: (i, 0, 0)),
        ),
        out_shape=jax.ShapeDtypeStruct((rows, cols, NT), F32),
        cost_estimate=pl.CostEstimate(
            flops=12 * rows * cols * NT * NT, bytes_accessed=8 * rows * cols * NT, transcendentals=0
        ),
        name="inverse",
    )(core, jnp.asarray(w), *ms)


def plain(recorded, panels):
    forth, back = (jnp.asarray(x, F32) for x in tables())
    best = lax.Precision.HIGHEST
    to_bins = lambda x: lax.all_to_all(
        jnp.einsum("fct,abt->fcab", forth, x, precision=best), "freq", split_axis=0, concat_axis=3, tiled=True
    )
    d = to_bins(recorded)
    g = lax.all_gather(to_bins(panels), "src", axis=2, tiled=True)
    mul = functools.partial(jnp.einsum, "fik,fkr->fir", precision=best)
    re = mul(d[:, 0], g[:, 0]) - mul(d[:, 1], g[:, 1])
    im = mul(d[:, 0], g[:, 1]) + mul(d[:, 1], g[:, 0])
    m = lax.all_to_all(jnp.stack([re, im], axis=1), "freq", split_axis=3, concat_axis=0, tiled=True)
    return jnp.einsum("fcir,fct->irt", m, back, precision=best)


def local(around, along, recorded, panels):
    tiled = all(x.shape[1] % 128 == 0 and x.shape[0] % 32 == 0 for x in (recorded, panels))
    if around != 4 or along != 8 or not tiled:
        return plain(recorded, panels)
    half = NF // 2
    levels = along // 2
    ring = list(range(around // 2)) + list(range(around - 1, around // 2 - 1, -1))
    clockwise = [(ring[i], ring[(i + 1) % around]) for i in range(around)]
    counter = [(b, a) for a, b in clockwise]
    upward = [(2 * z + c, 2 * z + 2 + c) for z in range(levels - 1) for c in range(2)]
    downward = [(b, a) for a, b in upward]
    partner = [(i, i ^ 1) for i in range(along)]

    me_ring, me_src = lax.axis_index("freq"), lax.axis_index("src")
    core, z = me_src % 2, me_src // 2
    at = jnp.where(me_ring < around // 2, me_ring, around // 2 + around - 1 - me_ring)
    core_at = core.astype(jnp.int32).reshape(1)
    bins = bins_of(half)
    chunks = len(bins)
    where = jnp.asarray(np.argsort(ring), jnp.int32)
    slot = ((at - where[(z - jnp.arange(levels)) % levels]) % around).astype(jnp.int32)
    me = (slot, core.astype(jnp.int32), z)
    edges = [int(e) for e in np.cumsum([0] + [2 * b for b in bins])]
    cuts = list(zip(edges[:-1], edges[1:]))
    cuts += [(NF + a, NF + b) for a, b in cuts]

    def transform(*args):
        return list(forward(*args))

    n = recorded.shape[0]
    ahead = n // 4
    head = transform(recorded, core_at, cuts[:1], 0, ahead)
    g_parts = transform(panels, core_at, cuts[:1])
    d_parts = transform(recorded, core_at, cuts[:1], ahead, n - ahead)
    g_parts += transform(panels, core_at, cuts[1:])
    d_parts += transform(recorded, core_at, cuts[1:])
    ms = []
    for c in range(chunks):
        g_own = [g_parts[c], lax.ppermute(g_parts[chunks + c], "src", partner)]
        d_swapped = lax.ppermute(d_parts[chunks + c], "src", partner)
        d_own = [d_parts[c], d_swapped] if c else head + [d_parts[c], d_swapped]
        if c:
            g_own = [jnp.stack(g_own)]
        g = {("own", 0): g_own}
        up, down = g_own, g_own
        for s in range(1, levels):
            up = [lax.ppermute(x, "src", upward) for x in up]
            down = [lax.ppermute(x, "src", downward) for x in down]
            g["up", s], g["down", s] = up, down
        d = {0: d_own}
        right, left = d_own, d_own
        for a in range(1, around // 2):
            right = [lax.ppermute(x, "freq", clockwise) for x in right]
            left = [lax.ppermute(x, "freq", counter) for x in left]
            d[a], d[around - a] = right, left
        last = around // 2
        mine = len(d_own) - 1
        d[last] = [lax.ppermute(x, "freq", clockwise) for x in right[:mine]]
        d[last].append(lax.ppermute(left[mine], "freq", counter))
        if c < chunks - 1:
            m = product(ALL, me, d, g)
        else:
            m = product(EARLY, me, d, g)
            m = product(LATE, me, d, g, m)
        ms.append([m[0], lax.ppermute(m[1], "src", partner)])
    return inverse([m[0] for m in ms] + [m[1] for m in ms], core_at)


def solution(mesh):
    return jax.shard_map(
        functools.partial(local, mesh.shape["freq"], mesh.shape["src"]),
        mesh=mesh,
        in_specs=(P("src", "freq", None), P("src", "freq", None)),
        out_specs=P("src", "freq", None),
        check_vma=False,
    )
```

```python
import functools

import jax
import jax.numpy as jnp
import ml_dtypes
import numpy as np
from jax import lax
from jax.experimental import pallas as pl
from jax.experimental.pallas import tpu as pltpu
from jax.sharding import PartitionSpec as P


NT = 128
NF = 64
SPLIT = (1,)
SHARES = (20, 12)
GRANT = 53 << 20
F32, BF16 = jnp.float32, jnp.bfloat16


def tables():
    phase = np.arange(NF)[:, None] * np.arange(NT)[None, :] % NT
    angle = 2.0 * np.pi / NT * phase
    forward = np.stack([np.cos(angle), -np.sin(angle)], axis=1)
    weight = np.where(np.arange(NF) == 0, 1.0, 2.0) / NT
    return forward, forward * weight[:, None, None]


def by_core(table):
    half = NF // 2
    low, high = table[:half].reshape(NF, NT), table[half:].reshape(NF, NT)
    return np.stack([np.concatenate([low, high]), np.concatenate([high, low])])


def parts(table):
    high = table.astype(ml_dtypes.bfloat16)
    low = (table - high.astype(np.float64)).astype(ml_dtypes.bfloat16)
    return high, low


def split(x):
    high = x.astype(BF16)
    return high, (x - high.astype(F32)).astype(BF16)


def bins_of(half):
    return tuple(half * share // sum(SHARES) for share in SHARES)


def forward_kernel(counts, core_ref, w_ref, x_ref, *out_refs):
    rows, m, t = x_ref.shape
    group = 8

    def some(q, carry):
        first = pl.multiple_of(q * group, group)
        high, low = split(x_ref[pl.ds(first, group)].reshape(group * m, t))
        x = jnp.concatenate([high, low], axis=1)
        both = lax.dot_general(w_ref[0], x, (((1,), (1,)), ((), ())), preferred_element_type=F32)
        n = both.shape[0] // 2
        res = both[:n] + both[n:]
        at = 0
        for out, count in zip(out_refs, counts):
            view = out.at[:, pl.ds(first, group), :]
            for i in range(group):
                view[:, i, :] = res[at : at + count, i * m : (i + 1) * m]
            at += count
        return carry

    lax.fori_loop(0, rows // group, some, 0)


def forward(x, core, cuts, start=0, n=None):
    m, t = x.shape[1:]
    n = x.shape[0] if n is None else n
    table = by_core(tables()[0])
    table = np.concatenate([table[:, a:b] for a, b in cuts], axis=1)
    counts = [b - a for a, b in cuts]
    shapes = [jax.ShapeDtypeStruct((count, n, m), F32) for count in counts]
    high, low = parts(table)
    w = np.concatenate(
        [np.concatenate([high, high], axis=2), np.concatenate([low, np.zeros_like(low)], axis=2)], axis=1
    )
    step = 32 if n > 64 else 16
    return pl.pallas_call(
        functools.partial(forward_kernel, counts),
        grid_spec=pltpu.PrefetchScalarGridSpec(
            num_scalar_prefetch=1,
            grid=(n // step,),
            in_specs=[
                pl.BlockSpec((1,) + w.shape[1:], lambda i, c: (c[0], 0, 0)),
                pl.BlockSpec((step, m, t), lambda i, c: (i + start // step, 0, 0)),
            ],
            out_specs=[pl.BlockSpec((s.shape[0], step, m), lambda i, c: (0, i, 0)) for s in shapes],
        ),
        out_shape=shapes,
        cost_estimate=pl.CostEstimate(
            flops=12 * n * m * t * NT, bytes_accessed=8 * n * m * t, transcendentals=0
        ),
        name="forward",
    )(core, jnp.asarray(w), x)


ALL, EARLY, LATE = range(3)


def sides(part, levels):
    pairs = [[("own", 0)]] + [[("up", s), ("down", levels - s)] for s in range(1, levels)]
    return [[x for x in pair if part != EARLY or x[1] < levels - 1] for pair in pairs]


def product_kernel(part, levels, places, d_keys, g_keys, slot_ref, *refs):
    d_refs = {}
    for (a, at), ref in zip(d_keys, refs):
        d_refs.setdefault(a, []).append((at, ref))
    g_refs = {}
    for (way, hop, h), ref in zip(g_keys, refs[len(d_keys) :]):
        for i in range(2) if h is None else (h,):
            g_refs[way, hop, i] = ref.at[i] if h is None else ref
    rest = refs[len(d_keys) + len(g_keys) :]
    lhs, rhs = rest[-2:]
    count = refs[0].shape[0] // 2
    depth = refs[0].shape[2]
    rows = lhs.shape[1] // 4
    half, cols = next(iter(g_refs.values())).shape[1:]
    core, chosen, far = (slot_ref[levels + i] for i in range(3))
    step, each = pl.program_id(0), 4 // count

    def put_g(b, slot, h, half_of, g):
        high, low = split(g)
        place = jnp.where(core == h, 0, half)
        at = pl.multiple_of(slot * 3 * depth + place, half)
        to = slice(half_of * cols, (half_of + 1) * cols)
        for i, value in enumerate((high, high, low)):
            rhs[b % 2, pl.ds(at + i * depth, half), to] = value

    def put_d(b, place, which):
        for i, (at, ref) in enumerate(d_refs[which[0]]):
            for half_of in range(2):
                value = ref[2 * b + half_of]
                for a in which[1:]:
                    value = jnp.where(chosen == a, d_refs[a][i][1][2 * b + half_of], value)
                high, low = split(value)
                first = 2 * rows * half_of + at
                for j, piece in enumerate((high, low, high)):
                    to = slice((3 * place + j) * depth, (3 * place + j + 1) * depth)
                    lhs[b % 2, first : first + ref.shape[1], to] = piece

    for b in range(count):
        for h in range(2):
            for half_of in range(2):
                row = 2 * b + half_of
                blocks = [sum(g_refs[way, hop, h][row] for way, hop in pair) for pair in sides(part, levels)]
                if part == LATE:
                    met = blocks[0]
                    for s in range(1, levels):
                        met = jnp.where(slot_ref[s] == 0, blocks[s], met)
                    last = g_refs["up", levels - 1, h][row] + g_refs["down", levels - 1, h][row]
                    put_g(b, 0, h, half_of, met)
                    put_g(b, 1, h, half_of, jnp.where(far > 0, last, 0.0))
                else:
                    for s, block in enumerate(blocks):
                        put_g(b, slot_ref[s], h, half_of, block)
        for place, which in enumerate(places):
            put_d(b, place, which)
        deep = 3 * depth * len(places)
        p = jnp.dot(lhs[b % 2, :, :deep], rhs[b % 2, :deep, :], preferred_element_type=F32)
        real = p[: 2 * rows, :cols] - p[2 * rows :, cols:]
        imaginary = p[: 2 * rows, cols:] + p[2 * rows :, :cols]
        if part == EARLY:
            rest[0][2 * b], rest[0][2 * b + 1] = real, imaginary
            continue
        if part == LATE:
            real, imaginary = real + rest[0][2 * b], imaginary + rest[0][2 * b + 1]
        held = rest[-3]
        row = 2 * (step % each * count + b)
        held[row], held[row + 1] = real, imaginary

    if part != EARLY:

        @pl.when(step % each == each - 1)
        def _():
            out_a, out_b, held = rest[-5:-2]
            for c in range(held.shape[0]):
                out_a[:, c, :] = held[c, :rows]
                out_b[:, c, :] = held[c, rows:]


def numbers(part, me, d, g):
    slot, core, z = me
    levels = slot.shape[0]
    around = len(d)
    diag = around // 2
    far_a = slot[jnp.where(z == 0, 1, levels - 1)]
    far = ((z == 0) | (z == levels - 1)) & (far_a != diag)
    chosen = jnp.where(far, far_a, 0)
    others = [a for a in range(around) if a != diag]
    if part == ALL:
        places, to = [[a] for a in range(around)], slot
    elif part == EARLY:
        places, to = [[a] for a in others], jnp.where(slot == diag, len(others), slot - (slot > diag))
    else:
        places, to = [[diag], others], jnp.where(slot == diag, 0, 2)
    needed = []
    for a in sorted(set(sum(places, []))):
        needed += [chosen == a if part == LATE and a != diag else True] * d[a]
    for s, pair in enumerate(sides(part, levels)):
        for way, hop in pair:
            there = {"own": True, "up": z >= hop, "down": z + hop < levels}[way]
            if part == LATE:
                there = there & ((slot[s] == diag) | (hop == levels - 1))
            needed += [there] * g
    needed.append(True)
    scalars = [core, chosen, far] + needed
    scalars = [to.astype(jnp.int32), jnp.stack([jnp.asarray(x).astype(jnp.int32) for x in scalars])]
    return places, jnp.concatenate(scalars)


def product(part, places, scalars, d, g, so_far=None):
    levels = 1 + max(hop for _, hop in g)
    depth = d[0][0].shape[2]
    n = d[0][0].shape[0]
    rows = sum(x.shape[1] for x in d[0]) // 2
    _, cols = g["own", 0][0].shape[-2:]
    step = 4
    operands, d_keys, g_keys = [], [], []
    for a in sorted(set(sum(places, []))):
        at = 0
        for x in d[a]:
            d_keys.append((a, at))
            operands.append(x)
            at += x.shape[1]
    for pair in sides(part, levels):
        for way, hop in pair:
            for h, x in enumerate(g[way, hop]):
                g_keys.append((way, hop, h if len(g[way, hop]) == 2 else None))
                operands.append(x)
    if so_far is not None:
        operands.append(so_far)
    first = levels + 3

    def spec(i, x):
        at = lambda j, c: jnp.where(c[first + i] > 0, j, 0)
        if x.ndim == 4:
            return pl.BlockSpec((2, step) + x.shape[2:], lambda j, c: (0, at(j, c), 0, 0))
        return pl.BlockSpec((step,) + x.shape[1:], lambda j, c: (at(j, c), 0, 0))

    scratch = [
        pltpu.VMEM((2, 4 * rows, 3 * depth * len(places)), BF16),
        pltpu.VMEM((2, 3 * depth * (len(places) + 1), 2 * cols), BF16),
    ]
    if part == EARLY:
        out = jax.ShapeDtypeStruct((n, 2 * rows, cols), F32)
        out_specs = pl.BlockSpec((step, 2 * rows, cols), lambda i, c: (i, 0, 0))
    else:
        out = [jax.ShapeDtypeStruct((rows, n, cols), F32)] * 2
        out_specs = [pl.BlockSpec((rows, 8, cols), lambda i, c: (0, i * step // 8, 0))] * 2
        scratch = [pltpu.VMEM((8, 2 * rows, cols), F32)] + scratch
    return pl.pallas_call(
        functools.partial(product_kernel, part, levels, places, d_keys, g_keys),
        grid_spec=pltpu.PrefetchScalarGridSpec(
            num_scalar_prefetch=1,
            grid=(n // step,),
            in_specs=[spec(i, x) for i, x in enumerate(operands)],
            out_specs=out_specs,
            scratch_shapes=scratch,
        ),
        out_shape=out,
        compiler_params=pltpu.CompilerParams(vmem_limit_bytes=GRANT if part == LATE else None),
        cost_estimate=pl.CostEstimate(
            flops=n // 2 * 2 * 4 * rows * 3 * len(places) * depth * 2 * cols,
            bytes_accessed=4 * sum(x.size for x in operands),
            transcendentals=0,
        ),
    )(scalars, *operands)


def inverse_kernel(count, core_ref, w_ref, *refs):
    x_refs, out = refs[:count], refs[-1]
    group = 8

    def some(q, carry):
        for u in range(group):
            i = q * group + u
            high, low = split(jnp.concatenate([x[i] for x in x_refs], axis=0))
            x = jnp.concatenate([high, low], axis=0)
            both = lax.dot_general(x, w_ref[0], (((0,), (0,)), ((), ())), preferred_element_type=F32)
            res = both[:, :NT] + both[:, NT:]
            out[i] = res if len(refs) == count + 1 else res + refs[count][i]
        return carry

    lax.fori_loop(0, out.shape[0] // group, some, 0)


def inverse(ms, core, cuts, so_far=None):
    rows, _, cols = ms[0].shape
    table = by_core(tables()[1])
    high, low = parts(np.concatenate([table[:, a:b] for a, b in cuts], axis=1))
    operands = list(ms) + ([] if so_far is None else [so_far])
    w = np.concatenate(
        [np.concatenate([high, low], axis=2), np.concatenate([high, np.zeros_like(low)], axis=2)], axis=1
    )
    step = 32
    return pl.pallas_call(
        functools.partial(inverse_kernel, len(ms)),
        grid_spec=pltpu.PrefetchScalarGridSpec(
            num_scalar_prefetch=1,
            grid=(rows // step,),
            in_specs=[pl.BlockSpec((1,) + w.shape[1:], lambda i, c: (c[0], 0, 0))]
            + [pl.BlockSpec((step,) + x.shape[1:], lambda i, c: (i, 0, 0)) for x in operands],
            out_specs=pl.BlockSpec((step, cols, NT), lambda i, c: (i, 0, 0)),
        ),
        out_shape=jax.ShapeDtypeStruct((rows, cols, NT), F32),
        compiler_params=pltpu.CompilerParams(vmem_limit_bytes=GRANT),
        cost_estimate=pl.CostEstimate(
            flops=12 * rows * cols * NT * NT, bytes_accessed=8 * rows * cols * NT, transcendentals=0
        ),
        name="inverse",
    )(core, jnp.asarray(w), *operands)


def plain(recorded, panels):
    forth, back = (jnp.asarray(x, F32) for x in tables())
    best = lax.Precision.HIGHEST
    to_bins = lambda x: lax.all_to_all(
        jnp.einsum("fct,abt->fcab", forth, x, precision=best), "freq", split_axis=0, concat_axis=3, tiled=True
    )
    d = to_bins(recorded)
    g = lax.all_gather(to_bins(panels), "src", axis=2, tiled=True)
    mul = functools.partial(jnp.einsum, "fik,fkr->fir", precision=best)
    re = mul(d[:, 0], g[:, 0]) - mul(d[:, 1], g[:, 1])
    im = mul(d[:, 0], g[:, 1]) + mul(d[:, 1], g[:, 0])
    m = lax.all_to_all(jnp.stack([re, im], axis=1), "freq", split_axis=3, concat_axis=0, tiled=True)
    return jnp.einsum("fcir,fct->irt", m, back, precision=best)


def local(around, along, recorded, panels):
    tiled = all(x.shape[1] % 128 == 0 and x.shape[0] % 32 == 0 for x in (recorded, panels))
    if around != 4 or along != 8 or not tiled:
        return plain(recorded, panels)
    half = NF // 2
    levels = along // 2
    ring = list(range(around // 2)) + list(range(around - 1, around // 2 - 1, -1))
    clockwise = [(ring[i], ring[(i + 1) % around]) for i in range(around)]
    counter = [(b, a) for a, b in clockwise]
    upward = [(2 * z + c, 2 * z + 2 + c) for z in range(levels - 1) for c in range(2)]
    downward = [(b, a) for a, b in upward]
    partner = [(i, i ^ 1) for i in range(along)]

    me_ring, me_src = lax.axis_index("freq"), lax.axis_index("src")
    core, z = me_src % 2, me_src // 2
    at = jnp.where(me_ring < around // 2, me_ring, around // 2 + around - 1 - me_ring)
    core_at = core.astype(jnp.int32).reshape(1)
    bins = bins_of(half)
    chunks = len(bins)
    where = jnp.asarray(np.argsort(ring), jnp.int32)
    slot = ((at - where[(z - jnp.arange(levels)) % levels]) % around).astype(jnp.int32)
    me = (slot, core.astype(jnp.int32), z)
    edges = [int(e) for e in np.cumsum([0] + [2 * b for b in bins])]
    cuts = list(zip(edges[:-1], edges[1:]))
    cuts += [(NF + a, NF + b) for a, b in cuts]

    def transform(*args):
        return list(forward(*args))

    n = recorded.shape[0]
    ahead = n // 4
    head = transform(recorded, core_at, cuts[:1], 0, ahead)
    g_parts = transform(panels, core_at, cuts[:1])
    d_parts = transform(recorded, core_at, cuts[:1], ahead, n - ahead)
    g_parts += transform(panels, core_at, cuts[1:])
    d_parts += transform(recorded, core_at, cuts[1:])
    ms = []
    for c in range(chunks):
        g_own = [g_parts[c], lax.ppermute(g_parts[chunks + c], "src", partner)]
        d_swapped = lax.ppermute(d_parts[chunks + c], "src", partner)
        d_own = [d_parts[c], d_swapped] if c else head + [d_parts[c], d_swapped]
        calls = (EARLY, LATE) if c in SPLIT else (ALL,)
        counts = {a: len(d_own) for a in range(around)}
        plans = [numbers(part, me, counts, 1 if c else 2) for part in calls]
        if c:
            g_own = [jnp.stack(g_own)]
        g = {("own", 0): g_own}
        up, down = g_own, g_own
        for s in range(1, levels):
            if s == 2:
                made, up[0] = lax.optimization_barrier(([x[1] for x in plans], up[0]))
                plans = [(x[0], y) for x, y in zip(plans, made)]
            up = [lax.ppermute(x, "src", upward) for x in up]
            down = [lax.ppermute(x, "src", downward) for x in down]
            g["up", s], g["down", s] = up, down
        d = {0: d_own}
        right, left = d_own, d_own
        for a in range(1, around // 2):
            right = [lax.ppermute(x, "freq", clockwise) for x in right]
            left = [lax.ppermute(x, "freq", counter) for x in left]
            d[a], d[around - a] = right, left
        last = around // 2
        mine = len(d_own) - 1
        d[last] = [lax.ppermute(x, "freq", clockwise) for x in right[:mine]]
        d[last].append(lax.ppermute(left[mine], "freq", counter))
        m = None
        for part, (places, scalars) in zip(calls, plans):
            m = product(part, places, scalars, d, g, m)
        ms.append([m[0], lax.ppermute(m[1], "src", partner)])
    acc = inverse(ms[0], core_at, [cuts[0], cuts[chunks]])
    return inverse(ms[1], core_at, [cuts[1], cuts[chunks + 1]], acc)


def solution(mesh):
    return jax.shard_map(
        functools.partial(local, mesh.shape["freq"], mesh.shape["src"]),
        mesh=mesh,
        in_specs=(P("src", "freq", None), P("src", "freq", None)),
        out_specs=P("src", "freq", None),
        check_vma=False,
    )
```

```python
import functools

import jax
import jax.numpy as jnp
import ml_dtypes
import numpy as np
from jax import lax
from jax.experimental import pallas as pl
from jax.experimental.pallas import tpu as pltpu
from jax.sharding import PartitionSpec as P


NT = 128
NF = 64
SPLIT = (0, 1)
SHARES = (20, 12)
GRANT = 50 << 20
F32, BF16 = jnp.float32, jnp.bfloat16


def tables():
    phase = np.arange(NF)[:, None] * np.arange(NT)[None, :] % NT
    angle = 2.0 * np.pi / NT * phase
    forward = np.stack([np.cos(angle), -np.sin(angle)], axis=1)
    weight = np.where(np.arange(NF) == 0, 1.0, 2.0) / NT
    return forward, forward * weight[:, None, None]


def by_core(table):
    half = NF // 2
    low, high = table[:half].reshape(NF, NT), table[half:].reshape(NF, NT)
    return np.stack([np.concatenate([low, high]), np.concatenate([high, low])])


def parts(table):
    high = table.astype(ml_dtypes.bfloat16)
    low = (table - high.astype(np.float64)).astype(ml_dtypes.bfloat16)
    return high, low


def split(x):
    high = x.astype(BF16)
    return high, (x - high.astype(F32)).astype(BF16)


def bins_of(half):
    return tuple(half * share // sum(SHARES) for share in SHARES)


def forward_kernel(counts, core_ref, w_ref, x_ref, *out_refs):
    rows, m, t = x_ref.shape
    group = 8

    def some(q, carry):
        first = pl.multiple_of(q * group, group)
        high, low = split(x_ref[pl.ds(first, group)].reshape(group * m, t))
        x = jnp.concatenate([high, low], axis=1)
        both = lax.dot_general(w_ref[0], x, (((1,), (1,)), ((), ())), preferred_element_type=F32)
        n = both.shape[0] // 2
        res = both[:n] + both[n:]
        at = 0
        for out, count in zip(out_refs, counts):
            view = out.at[:, pl.ds(first, group), :]
            for i in range(group):
                view[:, i, :] = res[at : at + count, i * m : (i + 1) * m]
            at += count
        return carry

    lax.fori_loop(0, rows // group, some, 0)


def forward(x, core, cuts, start=0, n=None):
    m, t = x.shape[1:]
    n = x.shape[0] if n is None else n
    table = by_core(tables()[0])
    table = np.concatenate([table[:, a:b] for a, b in cuts], axis=1)
    counts = [b - a for a, b in cuts]
    shapes = [jax.ShapeDtypeStruct((count, n, m), F32) for count in counts]
    high, low = parts(table)
    w = np.concatenate(
        [np.concatenate([high, high], axis=2), np.concatenate([low, np.zeros_like(low)], axis=2)], axis=1
    )
    step = 32 if n > 64 else 16
    return pl.pallas_call(
        functools.partial(forward_kernel, counts),
        grid_spec=pltpu.PrefetchScalarGridSpec(
            num_scalar_prefetch=1,
            grid=(n // step,),
            in_specs=[
                pl.BlockSpec((1,) + w.shape[1:], lambda i, c: (c[0], 0, 0)),
                pl.BlockSpec((step, m, t), lambda i, c: (i + start // step, 0, 0)),
            ],
            out_specs=[pl.BlockSpec((s.shape[0], step, m), lambda i, c: (0, i, 0)) for s in shapes],
        ),
        out_shape=shapes,
        cost_estimate=pl.CostEstimate(
            flops=12 * n * m * t * NT, bytes_accessed=8 * n * m * t, transcendentals=0
        ),
        name="forward",
    )(core, jnp.asarray(w), x)


ALL, EARLY, LATE = range(3)


def sides(part, levels):
    pairs = [[("own", 0)]] + [[("up", s), ("down", levels - s)] for s in range(1, levels)]
    return [[x for x in pair if part != EARLY or x[1] < levels - 1] for pair in pairs]


def product_kernel(part, levels, places, d_keys, g_keys, slot_ref, *refs):
    d_refs = {}
    for (a, at), ref in zip(d_keys, refs):
        d_refs.setdefault(a, []).append((at, ref))
    g_refs = {}
    for (way, hop, h), ref in zip(g_keys, refs[len(d_keys) :]):
        for i in range(2) if h is None else (h,):
            g_refs[way, hop, i] = ref.at[i] if h is None else ref
    rest = refs[len(d_keys) + len(g_keys) :]
    lhs, rhs = rest[-2:]
    count = refs[0].shape[0] // 2
    depth = refs[0].shape[2]
    rows = lhs.shape[1] // 4
    half, cols = next(iter(g_refs.values())).shape[1:]
    core, chosen, far = (slot_ref[levels + i] for i in range(3))
    step, each = pl.program_id(0), 4 // count

    def put_g(b, slot, h, half_of, g):
        high, low = split(g)
        place = jnp.where(core == h, 0, half)
        at = pl.multiple_of(slot * 3 * depth + place, half)
        to = slice(half_of * cols, (half_of + 1) * cols)
        for i, value in enumerate((high, high, low)):
            rhs[b % 2, pl.ds(at + i * depth, half), to] = value

    def put_d(b, place, which):
        for i, (at, ref) in enumerate(d_refs[which[0]]):
            for half_of in range(2):
                value = ref[2 * b + half_of]
                for a in which[1:]:
                    value = jnp.where(chosen == a, d_refs[a][i][1][2 * b + half_of], value)
                high, low = split(value)
                first = 2 * rows * half_of + at
                for j, piece in enumerate((high, low, high)):
                    to = slice((3 * place + j) * depth, (3 * place + j + 1) * depth)
                    lhs[b % 2, first : first + ref.shape[1], to] = piece

    for b in range(count):
        for h in range(2):
            for half_of in range(2):
                row = 2 * b + half_of
                blocks = [sum(g_refs[way, hop, h][row] for way, hop in pair) for pair in sides(part, levels)]
                if part == LATE:
                    met = blocks[0]
                    for s in range(1, levels):
                        met = jnp.where(slot_ref[s] == 0, blocks[s], met)
                    last = g_refs["up", levels - 1, h][row] + g_refs["down", levels - 1, h][row]
                    put_g(b, 0, h, half_of, met)
                    put_g(b, 1, h, half_of, jnp.where(far > 0, last, 0.0))
                else:
                    for s, block in enumerate(blocks):
                        put_g(b, slot_ref[s], h, half_of, block)
        for place, which in enumerate(places):
            put_d(b, place, which)
        deep = 3 * depth * len(places)
        p = jnp.dot(lhs[b % 2, :, :deep], rhs[b % 2, :deep, :], preferred_element_type=F32)
        real = p[: 2 * rows, :cols] - p[2 * rows :, cols:]
        imaginary = p[: 2 * rows, cols:] + p[2 * rows :, :cols]
        if part == EARLY:
            rest[0][2 * b], rest[0][2 * b + 1] = real, imaginary
            continue
        if part == LATE:
            real, imaginary = real + rest[0][2 * b], imaginary + rest[0][2 * b + 1]
        held = rest[-3]
        row = 2 * (step % each * count + b)
        held[row], held[row + 1] = real, imaginary

    if part != EARLY:

        @pl.when(step % each == each - 1)
        def _():
            out_a, out_b, held = rest[-5:-2]
            for c in range(held.shape[0]):
                out_a[:, c, :] = held[c, :rows]
                out_b[:, c, :] = held[c, rows:]


def numbers(part, me, d, g):
    slot, core, z = me
    levels = slot.shape[0]
    around = len(d)
    diag = around // 2
    far_a = slot[jnp.where(z == 0, 1, levels - 1)]
    far = ((z == 0) | (z == levels - 1)) & (far_a != diag)
    chosen = jnp.where(far, far_a, 0)
    others = [a for a in range(around) if a != diag]
    if part == ALL:
        places, to = [[a] for a in range(around)], slot
    elif part == EARLY:
        places, to = [[a] for a in others], jnp.where(slot == diag, len(others), slot - (slot > diag))
    else:
        places, to = [[diag], others], jnp.where(slot == diag, 0, 2)
    needed = []
    for a in sorted(set(sum(places, []))):
        needed += [chosen == a if part == LATE and a != diag else True] * d[a]
    for s, pair in enumerate(sides(part, levels)):
        for way, hop in pair:
            there = {"own": True, "up": z >= hop, "down": z + hop < levels}[way]
            if part == LATE:
                there = there & ((slot[s] == diag) | (hop == levels - 1))
            needed += [there] * g
    needed.append(True)
    scalars = [core, chosen, far] + needed
    scalars = [to.astype(jnp.int32), jnp.stack([jnp.asarray(x).astype(jnp.int32) for x in scalars])]
    return places, jnp.concatenate(scalars)


def product(part, places, scalars, d, g, so_far=None):
    levels = 1 + max(hop for _, hop in g)
    depth = d[0][0].shape[2]
    n = d[0][0].shape[0]
    rows = sum(x.shape[1] for x in d[0]) // 2
    _, cols = g["own", 0][0].shape[-2:]
    step = 4
    operands, d_keys, g_keys = [], [], []
    for a in sorted(set(sum(places, []))):
        at = 0
        for x in d[a]:
            d_keys.append((a, at))
            operands.append(x)
            at += x.shape[1]
    for pair in sides(part, levels):
        for way, hop in pair:
            for h, x in enumerate(g[way, hop]):
                g_keys.append((way, hop, h if len(g[way, hop]) == 2 else None))
                operands.append(x)
    if so_far is not None:
        operands.append(so_far)
    first = levels + 3

    def spec(i, x):
        at = lambda j, c: jnp.where(c[first + i] > 0, j, 0)
        if x.ndim == 4:
            return pl.BlockSpec((2, step) + x.shape[2:], lambda j, c: (0, at(j, c), 0, 0))
        return pl.BlockSpec((step,) + x.shape[1:], lambda j, c: (at(j, c), 0, 0))

    scratch = [
        pltpu.VMEM((2, 4 * rows, 3 * depth * len(places)), BF16),
        pltpu.VMEM((2, 3 * depth * (len(places) + 1), 2 * cols), BF16),
    ]
    if part == EARLY:
        out = jax.ShapeDtypeStruct((n, 2 * rows, cols), F32)
        out_specs = pl.BlockSpec((step, 2 * rows, cols), lambda i, c: (i, 0, 0))
    else:
        out = [jax.ShapeDtypeStruct((rows, n, cols), F32)] * 2
        out_specs = [pl.BlockSpec((rows, 8, cols), lambda i, c: (0, i * step // 8, 0))] * 2
        scratch = [pltpu.VMEM((8, 2 * rows, cols), F32)] + scratch
    return pl.pallas_call(
        functools.partial(product_kernel, part, levels, places, d_keys, g_keys),
        grid_spec=pltpu.PrefetchScalarGridSpec(
            num_scalar_prefetch=1,
            grid=(n // step,),
            in_specs=[spec(i, x) for i, x in enumerate(operands)],
            out_specs=out_specs,
            scratch_shapes=scratch,
        ),
        out_shape=out,
        compiler_params=pltpu.CompilerParams(vmem_limit_bytes=GRANT if part == LATE else None),
        cost_estimate=pl.CostEstimate(
            flops=n // 2 * 2 * 4 * rows * 3 * len(places) * depth * 2 * cols,
            bytes_accessed=4 * sum(x.size for x in operands),
            transcendentals=0,
        ),
    )(scalars, *operands)


def inverse_kernel(count, core_ref, w_ref, *refs):
    x_refs, out = refs[:count], refs[-1]
    group = 8

    def some(q, carry):
        for u in range(group):
            i = q * group + u
            high, low = split(jnp.concatenate([x[i] for x in x_refs], axis=0))
            x = jnp.concatenate([high, low], axis=0)
            both = lax.dot_general(x, w_ref[0], (((0,), (0,)), ((), ())), preferred_element_type=F32)
            res = both[:, :NT] + both[:, NT:]
            out[i] = res if len(refs) == count + 1 else res + refs[count][i]
        return carry

    lax.fori_loop(0, out.shape[0] // group, some, 0)


def inverse(ms, core, cuts, so_far=None):
    rows, _, cols = ms[0].shape
    table = by_core(tables()[1])
    high, low = parts(np.concatenate([table[:, a:b] for a, b in cuts], axis=1))
    operands = list(ms) + ([] if so_far is None else [pltpu.with_memory_space_constraint(so_far, pltpu.VMEM)])
    w = np.concatenate(
        [np.concatenate([high, low], axis=2), np.concatenate([high, np.zeros_like(low)], axis=2)], axis=1
    )
    step = 32
    return pl.pallas_call(
        functools.partial(inverse_kernel, len(ms)),
        grid_spec=pltpu.PrefetchScalarGridSpec(
            num_scalar_prefetch=1,
            grid=(rows // step,),
            in_specs=[pl.BlockSpec((1,) + w.shape[1:], lambda i, c: (c[0], 0, 0))]
            + [pl.BlockSpec((step,) + x.shape[1:], lambda i, c: (i, 0, 0)) for x in operands],
            out_specs=pl.BlockSpec((step, cols, NT), lambda i, c: (i, 0, 0)),
        ),
        out_shape=(pltpu.VMEM if so_far is None else jax.ShapeDtypeStruct)((rows, cols, NT), F32),
        compiler_params=pltpu.CompilerParams(vmem_limit_bytes=GRANT - (12 << 20)),
        cost_estimate=pl.CostEstimate(
            flops=12 * rows * cols * NT * NT, bytes_accessed=8 * rows * cols * NT, transcendentals=0
        ),
        name="inverse",
    )(core, jnp.asarray(w), *operands)


def plain(recorded, panels):
    forth, back = (jnp.asarray(x, F32) for x in tables())
    best = lax.Precision.HIGHEST
    to_bins = lambda x: lax.all_to_all(
        jnp.einsum("fct,abt->fcab", forth, x, precision=best), "freq", split_axis=0, concat_axis=3, tiled=True
    )
    d = to_bins(recorded)
    g = lax.all_gather(to_bins(panels), "src", axis=2, tiled=True)
    mul = functools.partial(jnp.einsum, "fik,fkr->fir", precision=best)
    re = mul(d[:, 0], g[:, 0]) - mul(d[:, 1], g[:, 1])
    im = mul(d[:, 0], g[:, 1]) + mul(d[:, 1], g[:, 0])
    m = lax.all_to_all(jnp.stack([re, im], axis=1), "freq", split_axis=3, concat_axis=0, tiled=True)
    return jnp.einsum("fcir,fct->irt", m, back, precision=best)


def local(around, along, recorded, panels):
    tiled = all(x.shape[1] % 128 == 0 and x.shape[0] % 32 == 0 for x in (recorded, panels))
    if around != 4 or along != 8 or not tiled:
        return plain(recorded, panels)
    half = NF // 2
    levels = along // 2
    ring = list(range(around // 2)) + list(range(around - 1, around // 2 - 1, -1))
    clockwise = [(ring[i], ring[(i + 1) % around]) for i in range(around)]
    counter = [(b, a) for a, b in clockwise]
    upward = [(2 * z + c, 2 * z + 2 + c) for z in range(levels - 1) for c in range(2)]
    downward = [(b, a) for a, b in upward]
    partner = [(i, i ^ 1) for i in range(along)]

    me_ring, me_src = lax.axis_index("freq"), lax.axis_index("src")
    core, z = me_src % 2, me_src // 2
    at = jnp.where(me_ring < around // 2, me_ring, around // 2 + around - 1 - me_ring)
    core_at = core.astype(jnp.int32).reshape(1)
    bins = bins_of(half)
    chunks = len(bins)
    where = jnp.asarray(np.argsort(ring), jnp.int32)
    slot = ((at - where[(z - jnp.arange(levels)) % levels]) % around).astype(jnp.int32)
    me = (slot, core.astype(jnp.int32), z)
    edges = [int(e) for e in np.cumsum([0] + [2 * b for b in bins])]
    cuts = list(zip(edges[:-1], edges[1:]))
    cuts += [(NF + a, NF + b) for a, b in cuts]

    def transform(*args):
        return list(forward(*args))

    n = recorded.shape[0]
    ahead = n // 4
    head = transform(recorded, core_at, cuts[:1], 0, ahead)
    g_parts = transform(panels, core_at, cuts[:1])
    d_parts = transform(recorded, core_at, cuts[:1], ahead, n - ahead)
    g_parts += transform(panels, core_at, cuts[1:])
    d_parts += transform(recorded, core_at, cuts[1:])
    ms = []
    for c in range(chunks):
        g_own = [g_parts[c], lax.ppermute(g_parts[chunks + c], "src", partner)]
        d_swapped = lax.ppermute(d_parts[chunks + c], "src", partner)
        d_own = [d_parts[c], d_swapped] if c else head + [d_parts[c], d_swapped]
        calls = (EARLY, LATE) if c in SPLIT else (ALL,)
        counts = {a: len(d_own) for a in range(around)}
        plans = [numbers(part, me, counts, 1 if c else 2) for part in calls]
        if c:
            g_own = [jnp.stack(g_own)]
        g = {("own", 0): g_own}
        up, down = g_own, g_own
        for s in range(1, levels):
            if s == 2:
                made, up[0] = lax.optimization_barrier(([x[1] for x in plans], up[0]))
                plans = [(x[0], y) for x, y in zip(plans, made)]
            up = [lax.ppermute(x, "src", upward) for x in up]
            down = [lax.ppermute(x, "src", downward) for x in down]
            g["up", s], g["down", s] = up, down
        d = {0: d_own}
        right, left = d_own, d_own
        for a in range(1, around // 2):
            right = [lax.ppermute(x, "freq", clockwise) for x in right]
            left = [lax.ppermute(x, "freq", counter) for x in left]
            d[a], d[around - a] = right, left
        last = around // 2
        mine = len(d_own) - 1
        d[last] = [lax.ppermute(x, "freq", clockwise) for x in right[:mine]]
        d[last].append(lax.ppermute(left[mine], "freq", counter))
        m = None
        for part, (places, scalars) in zip(calls, plans):
            m = product(part, places, scalars, d, g, m)
        ms.append([m[0], lax.ppermute(m[1], "src", partner)])
    acc = inverse(ms[0], core_at, [cuts[0], cuts[chunks]])
    return inverse(ms[1], core_at, [cuts[1], cuts[chunks + 1]], acc)


def solution(mesh):
    return jax.shard_map(
        functools.partial(local, mesh.shape["freq"], mesh.shape["src"]),
        mesh=mesh,
        in_specs=(P("src", "freq", None), P("src", "freq", None)),
        out_specs=P("src", "freq", None),
        check_vma=False,
    )
```

```python
import functools

import jax
import jax.numpy as jnp
import ml_dtypes
import numpy as np
from jax import lax
from jax.experimental import pallas as pl
from jax.experimental.pallas import tpu as pltpu
from jax.sharding import PartitionSpec as P


NT = 128
NF = 64
SHARES = (20, 12)
SMALL = 4 << 20
GRANT = 46 << 20
F32, BF16 = jnp.float32, jnp.bfloat16


def tables():
    phase = np.arange(NF)[:, None] * np.arange(NT)[None, :] % NT
    angle = 2.0 * np.pi / NT * phase
    forward = np.stack([np.cos(angle), -np.sin(angle)], axis=1)
    weight = np.where(np.arange(NF) == 0, 1.0, 2.0) / NT
    return forward, forward * weight[:, None, None]


def by_core(table):
    half = NF // 2
    low, high = table[:half].reshape(NF, NT), table[half:].reshape(NF, NT)
    return np.stack([np.concatenate([low, high]), np.concatenate([high, low])])


def parts(table):
    high = table.astype(ml_dtypes.bfloat16)
    low = (table - high.astype(np.float64)).astype(ml_dtypes.bfloat16)
    return high, low


def split(x):
    high = x.astype(BF16)
    return high, (x - high.astype(F32)).astype(BF16)


def bins_of(half):
    return tuple(half * share // sum(SHARES) for share in SHARES)


def forward_kernel(counts, core_ref, w_ref, x_ref, *out_refs):
    rows, m, t = x_ref.shape
    group = 8

    def some(q, carry):
        first = pl.multiple_of(q * group, group)
        high, low = split(x_ref[pl.ds(first, group)].reshape(group * m, t))
        x = jnp.concatenate([high, low], axis=1)
        both = lax.dot_general(w_ref[0], x, (((1,), (1,)), ((), ())), preferred_element_type=F32)
        n = both.shape[0] // 2
        res = both[:n] + both[n:]
        at = 0
        for out, count in zip(out_refs, counts):
            view = out.at[:, pl.ds(first, group), :]
            for i in range(group):
                view[:, i, :] = res[at : at + count, i * m : (i + 1) * m]
            at += count
        return carry

    lax.fori_loop(0, rows // group, some, 0)


def forward(x, core, cuts, start=0, n=None):
    m, t = x.shape[1:]
    n = x.shape[0] if n is None else n
    table = by_core(tables()[0])
    table = np.concatenate([table[:, a:b] for a, b in cuts], axis=1)
    counts = [b - a for a, b in cuts]
    shapes = [jax.ShapeDtypeStruct((count, n, m), F32) for count in counts]
    high, low = parts(table)
    w = np.concatenate(
        [np.concatenate([high, high], axis=2), np.concatenate([low, np.zeros_like(low)], axis=2)], axis=1
    )
    step = 32 if n > 64 else 16
    return pl.pallas_call(
        functools.partial(forward_kernel, counts),
        grid_spec=pltpu.PrefetchScalarGridSpec(
            num_scalar_prefetch=1,
            grid=(n // step,),
            in_specs=[
                pl.BlockSpec((1,) + w.shape[1:], lambda i, c: (c[0], 0, 0)),
                pl.BlockSpec((step, m, t), lambda i, c: (i + start // step, 0, 0)),
            ],
            out_specs=[pl.BlockSpec((s.shape[0], step, m), lambda i, c: (0, i, 0)) for s in shapes],
        ),
        out_shape=shapes,
        cost_estimate=pl.CostEstimate(
            flops=12 * n * m * t * NT, bytes_accessed=8 * n * m * t, transcendentals=0
        ),
        name="forward",
    )(core, jnp.asarray(w), x)


ALL, EARLY, LATE, MIDDLE, FAR = range(5)
CALLS = ((EARLY, MIDDLE, FAR), (EARLY, LATE))


def sides(part, levels):
    pairs = [[("own", 0)]] + [[("up", s), ("down", levels - s)] for s in range(1, levels)]
    taken = {EARLY: lambda hop: hop < levels - 1, MIDDLE: lambda hop: hop < levels - 1, FAR: lambda hop: hop == levels - 1}
    return [[x for x in pair if taken.get(part, lambda hop: True)(x[1])] for pair in pairs]


def product_kernel(part, levels, places, d_keys, g_keys, slot_ref, *refs):
    d_refs = {}
    for (a, at), ref in zip(d_keys, refs):
        d_refs.setdefault(a, []).append((at, ref))
    g_refs = {}
    for (way, hop, h), ref in zip(g_keys, refs[len(d_keys) :]):
        for i in range(2) if h is None else (h,):
            g_refs[way, hop, i] = ref.at[i] if h is None else ref
    rest = refs[len(d_keys) + len(g_keys) :]
    lhs, rhs = rest[-2:]
    count = refs[0].shape[0] // 2
    depth = refs[0].shape[2]
    rows = lhs.shape[1] // 4
    half, cols = next(iter(g_refs.values())).shape[1:]
    core, chosen, far = (slot_ref[levels + i] for i in range(3))
    step, each = pl.program_id(0), 4 // count

    def put_g(b, slot, h, half_of, g):
        high, low = split(g)
        place = jnp.where(core == h, 0, half)
        at = pl.multiple_of(slot * 3 * depth + place, half)
        to = slice(half_of * cols, (half_of + 1) * cols)
        for i, value in enumerate((high, high, low)):
            rhs[b % 2, pl.ds(at + i * depth, half), to] = value

    def put_d(b, place, which):
        for i, (at, ref) in enumerate(d_refs[which[0]]):
            for half_of in range(2):
                value = ref[2 * b + half_of]
                for a in which[1:]:
                    value = jnp.where(chosen == a, d_refs[a][i][1][2 * b + half_of], value)
                high, low = split(value)
                first = 2 * rows * half_of + at
                for j, piece in enumerate((high, low, high)):
                    to = slice((3 * place + j) * depth, (3 * place + j + 1) * depth)
                    lhs[b % 2, first : first + ref.shape[1], to] = piece

    for b in range(count):
        for h in range(2):
            for half_of in range(2):
                row = 2 * b + half_of
                blocks = [sum(g_refs[way, hop, h][row] for way, hop in pair) for pair in sides(part, levels)]
                if part in (LATE, MIDDLE):
                    met = blocks[0]
                    for s in range(1, levels):
                        met = jnp.where(slot_ref[s] == 0, blocks[s], met)
                    put_g(b, 0, h, half_of, met)
                if part in (LATE, FAR):
                    last = g_refs["up", levels - 1, h][row] + g_refs["down", levels - 1, h][row]
                    put_g(b, len(places) - 1, h, half_of, jnp.where(far > 0, last, 0.0))
                if part in (ALL, EARLY):
                    for s, block in enumerate(blocks):
                        put_g(b, slot_ref[s], h, half_of, block)
        for place, which in enumerate(places):
            put_d(b, place, which)
        deep = 3 * depth * len(places)
        p = jnp.dot(lhs[b % 2, :, :deep], rhs[b % 2, :deep, :], preferred_element_type=F32)
        real = p[: 2 * rows, :cols] - p[2 * rows :, cols:]
        imaginary = p[: 2 * rows, cols:] + p[2 * rows :, :cols]
        if part not in (ALL, EARLY):
            real, imaginary = real + rest[0][2 * b], imaginary + rest[0][2 * b + 1]
        if part in (EARLY, MIDDLE):
            rest[-3][2 * b], rest[-3][2 * b + 1] = real, imaginary
            continue
        held = rest[-3]
        row = 2 * (step % each * count + b)
        held[row], held[row + 1] = real, imaginary

    if part not in (EARLY, MIDDLE):

        @pl.when(step % each == each - 1)
        def _():
            out_a, out_b, held = rest[-5:-2]
            for c in range(held.shape[0]):
                out_a[:, c, :] = held[c, :rows]
                out_b[:, c, :] = held[c, rows:]


def numbers(part, me, d, g):
    slot, core, z = me
    levels = slot.shape[0]
    around = len(d)
    diag = around // 2
    far_a = slot[jnp.where(z == 0, 1, levels - 1)]
    far = ((z == 0) | (z == levels - 1)) & ((far_a != diag) | (part == FAR))
    chosen = jnp.where(far, far_a, 0)
    others = [a for a in range(around) if a != diag]
    if part == ALL:
        places, to = [[a] for a in range(around)], slot
    elif part == EARLY:
        places, to = [[a] for a in others], jnp.where(slot == diag, len(others), slot - (slot > diag))
    elif part == FAR:
        places, to = [list(range(around))], slot
    else:
        places, to = [[diag], others][: 2 if part == LATE else 1], jnp.where(slot == diag, 0, 2)
    needed = []
    for a in sorted(set(sum(places, []))):
        picked = part == FAR or (part == LATE and a != diag)
        needed += [far & (chosen == a) if picked else True] * d[a]
    for s, pair in enumerate(sides(part, levels)):
        for way, hop in pair:
            there = {"own": True, "up": z >= hop, "down": z + hop < levels}[way]
            if part in (LATE, MIDDLE):
                there = there & ((slot[s] == diag) | (hop == levels - 1))
            needed += [there] * g
    needed.append(True)
    scalars = [core, chosen, far] + needed
    scalars = [to.astype(jnp.int32), jnp.stack([jnp.asarray(x).astype(jnp.int32) for x in scalars])]
    return places, jnp.concatenate(scalars)


def product(part, places, scalars, d, g, so_far=None):
    levels = 1 + max(hop for _, hop in g)
    raw = part in (EARLY, MIDDLE)
    depth = d[0][0].shape[2]
    n = d[0][0].shape[0]
    rows = sum(x.shape[1] for x in d[0]) // 2
    _, cols = g["own", 0][0].shape[-2:]
    step = 4
    operands, d_keys, g_keys = [], [], []
    for a in sorted(set(sum(places, []))):
        at = 0
        for x in d[a]:
            d_keys.append((a, at))
            operands.append(x)
            at += x.shape[1]
    for pair in sides(part, levels):
        for way, hop in pair:
            for h, x in enumerate(g[way, hop]):
                g_keys.append((way, hop, h if len(g[way, hop]) == 2 else None))
                operands.append(x)
    small = 8 * n * rows * cols <= SMALL
    if so_far is not None:
        operands.append(pltpu.with_memory_space_constraint(so_far, pltpu.VMEM) if small else so_far)
    first = levels + 3

    def spec(i, x):
        at = lambda j, c: jnp.where(c[first + i] > 0, j, 0)
        if x.ndim == 4:
            return pl.BlockSpec((2, step) + x.shape[2:], lambda j, c: (0, at(j, c), 0, 0))
        return pl.BlockSpec((step,) + x.shape[1:], lambda j, c: (at(j, c), 0, 0))

    scratch = [
        pltpu.VMEM((2, 4 * rows, 3 * depth * len(places)), BF16),
        pltpu.VMEM((2, 3 * depth * (len(places) + 1), 2 * cols), BF16),
    ]
    if raw:
        out = (pltpu.VMEM if small else jax.ShapeDtypeStruct)((n, 2 * rows, cols), F32)
        out_specs = pl.BlockSpec((step, 2 * rows, cols), lambda i, c: (i, 0, 0))
    else:
        out = [jax.ShapeDtypeStruct((rows, n, cols), F32)] * 2
        out_specs = [pl.BlockSpec((rows, 8, cols), lambda i, c: (0, i * step // 8, 0))] * 2
        scratch = [pltpu.VMEM((8, 2 * rows, cols), F32)] + scratch
    return pl.pallas_call(
        functools.partial(product_kernel, part, levels, places, d_keys, g_keys),
        grid_spec=pltpu.PrefetchScalarGridSpec(
            num_scalar_prefetch=1,
            grid=(n // step,),
            in_specs=[spec(i, x) for i, x in enumerate(operands)],
            out_specs=out_specs,
            scratch_shapes=scratch,
        ),
        out_shape=out,
        compiler_params=pltpu.CompilerParams(vmem_limit_bytes=GRANT if part == LATE and small else None),
        cost_estimate=pl.CostEstimate(
            flops=n // 2 * 2 * 4 * rows * 3 * len(places) * depth * 2 * cols,
            bytes_accessed=4 * sum(x.size for x in operands),
            transcendentals=0,
        ),
    )(scalars, *operands)


def inverse_kernel(count, core_ref, w_ref, *refs):
    x_refs, out = refs[:count], refs[-1]
    group = 8

    def some(q, carry):
        for u in range(group):
            i = q * group + u
            high, low = split(jnp.concatenate([x[i] for x in x_refs], axis=0))
            x = jnp.concatenate([high, low], axis=0)
            both = lax.dot_general(x, w_ref[0], (((0,), (0,)), ((), ())), preferred_element_type=F32)
            res = both[:, :NT] + both[:, NT:]
            out[i] = res if len(refs) == count + 1 else res + refs[count][i]
        return carry

    lax.fori_loop(0, out.shape[0] // group, some, 0)


def inverse(ms, core, cuts, so_far=None):
    rows, _, cols = ms[0].shape
    table = by_core(tables()[1])
    high, low = parts(np.concatenate([table[:, a:b] for a, b in cuts], axis=1))
    operands = list(ms) + ([] if so_far is None else [pltpu.with_memory_space_constraint(so_far, pltpu.VMEM)])
    w = np.concatenate(
        [np.concatenate([high, low], axis=2), np.concatenate([high, np.zeros_like(low)], axis=2)], axis=1
    )
    step = 32
    return pl.pallas_call(
        functools.partial(inverse_kernel, len(ms)),
        grid_spec=pltpu.PrefetchScalarGridSpec(
            num_scalar_prefetch=1,
            grid=(rows // step,),
            in_specs=[pl.BlockSpec((1,) + w.shape[1:], lambda i, c: (c[0], 0, 0))]
            + [pl.BlockSpec((step,) + x.shape[1:], lambda i, c: (i, 0, 0)) for x in operands],
            out_specs=pl.BlockSpec((step, cols, NT), lambda i, c: (i, 0, 0)),
        ),
        out_shape=(pltpu.VMEM if so_far is None else jax.ShapeDtypeStruct)((rows, cols, NT), F32),
        compiler_params=pltpu.CompilerParams(vmem_limit_bytes=GRANT - (8 << 20)),
        cost_estimate=pl.CostEstimate(
            flops=12 * rows * cols * NT * NT, bytes_accessed=8 * rows * cols * NT, transcendentals=0
        ),
        name="inverse",
    )(core, jnp.asarray(w), *operands)


def plain(recorded, panels):
    forth, back = (jnp.asarray(x, F32) for x in tables())
    best = lax.Precision.HIGHEST
    to_bins = lambda x: lax.all_to_all(
        jnp.einsum("fct,abt->fcab", forth, x, precision=best), "freq", split_axis=0, concat_axis=3, tiled=True
    )
    d = to_bins(recorded)
    g = lax.all_gather(to_bins(panels), "src", axis=2, tiled=True)
    mul = functools.partial(jnp.einsum, "fik,fkr->fir", precision=best)
    re = mul(d[:, 0], g[:, 0]) - mul(d[:, 1], g[:, 1])
    im = mul(d[:, 0], g[:, 1]) + mul(d[:, 1], g[:, 0])
    m = lax.all_to_all(jnp.stack([re, im], axis=1), "freq", split_axis=3, concat_axis=0, tiled=True)
    return jnp.einsum("fcir,fct->irt", m, back, precision=best)


def local(around, along, recorded, panels):
    tiled = all(x.shape[1] % 128 == 0 and x.shape[0] % 32 == 0 for x in (recorded, panels))
    if around != 4 or along != 8 or not tiled:
        return plain(recorded, panels)
    half = NF // 2
    levels = along // 2
    ring = list(range(around // 2)) + list(range(around - 1, around // 2 - 1, -1))
    clockwise = [(ring[i], ring[(i + 1) % around]) for i in range(around)]
    counter = [(b, a) for a, b in clockwise]
    upward = [(2 * z + c, 2 * z + 2 + c) for z in range(levels - 1) for c in range(2)]
    downward = [(b, a) for a, b in upward]
    partner = [(i, i ^ 1) for i in range(along)]

    me_ring, me_src = lax.axis_index("freq"), lax.axis_index("src")
    core, z = me_src % 2, me_src // 2
    at = jnp.where(me_ring < around // 2, me_ring, around // 2 + around - 1 - me_ring)
    core_at = core.astype(jnp.int32).reshape(1)
    bins = bins_of(half)
    chunks = len(bins)
    where = jnp.asarray(np.argsort(ring), jnp.int32)
    slot = ((at - where[(z - jnp.arange(levels)) % levels]) % around).astype(jnp.int32)
    me = (slot, core.astype(jnp.int32), z)
    edges = [int(e) for e in np.cumsum([0] + [2 * b for b in bins])]
    cuts = list(zip(edges[:-1], edges[1:]))
    cuts += [(NF + a, NF + b) for a, b in cuts]

    def transform(*args):
        return list(forward(*args))

    n = recorded.shape[0]
    ahead = n // 4
    head = transform(recorded, core_at, cuts[:1], 0, ahead)
    g_parts = transform(panels, core_at, cuts[:1])
    d_parts = transform(recorded, core_at, cuts[:1], ahead, n - ahead)
    g_parts += transform(panels, core_at, cuts[1:])
    d_parts += transform(recorded, core_at, cuts[1:])
    ms = []
    for c in range(chunks):
        g_own = [g_parts[c], lax.ppermute(g_parts[chunks + c], "src", partner)]
        d_swapped = lax.ppermute(d_parts[chunks + c], "src", partner)
        d_own = [d_parts[c], d_swapped] if c else head + [d_parts[c], d_swapped]
        calls = CALLS[c]
        counts = {a: len(d_own) for a in range(around)}
        plans = [numbers(part, me, counts, 1 if c else 2) for part in calls]
        if c:
            g_own = [jnp.stack(g_own)]
        g = {("own", 0): g_own}
        up, down = g_own, g_own
        for s in range(1, levels):
            if s == 2:
                made, up[0] = lax.optimization_barrier(([x[1] for x in plans], up[0]))
                plans = [(x[0], y) for x, y in zip(plans, made)]
            up = [lax.ppermute(x, "src", upward) for x in up]
            down = [lax.ppermute(x, "src", downward) for x in down]
            g["up", s], g["down", s] = up, down
        d = {0: d_own}
        right, left = d_own, d_own
        for a in range(1, around // 2):
            right = [lax.ppermute(x, "freq", clockwise) for x in right]
            left = [lax.ppermute(x, "freq", counter) for x in left]
            d[a], d[around - a] = right, left
        last = around // 2
        mine = len(d_own) - 1
        d[last] = [lax.ppermute(x, "freq", clockwise) for x in right[:mine]]
        d[last].append(lax.ppermute(left[mine], "freq", counter))
        m = None
        for part, (places, scalars) in zip(calls, plans):
            m = product(part, places, scalars, d, g, m)
        ms.append([m[0], lax.ppermute(m[1], "src", partner)])
    acc = inverse(ms[0], core_at, [cuts[0], cuts[chunks]])
    return inverse(ms[1], core_at, [cuts[1], cuts[chunks + 1]], acc)


def solution(mesh):
    return jax.shard_map(
        functools.partial(local, mesh.shape["freq"], mesh.shape["src"]),
        mesh=mesh,
        in_specs=(P("src", "freq", None), P("src", "freq", None)),
        out_specs=P("src", "freq", None),
        check_vma=False,
    )
```

```python
import functools

import jax
import jax.numpy as jnp
import ml_dtypes
import numpy as np
from jax import lax
from jax.experimental import pallas as pl
from jax.experimental.pallas import tpu as pltpu
from jax.sharding import PartitionSpec as P


NT = 128
NF = 64
SPLIT = (0, 1)
SHARES = (20, 12)
SMALL = 4 << 20
GRANT = 46 << 20
F32, BF16 = jnp.float32, jnp.bfloat16


def tables():
    phase = np.arange(NF)[:, None] * np.arange(NT)[None, :] % NT
    angle = 2.0 * np.pi / NT * phase
    forward = np.stack([np.cos(angle), -np.sin(angle)], axis=1)
    weight = np.where(np.arange(NF) == 0, 1.0, 2.0) / NT
    return forward, forward * weight[:, None, None]


def by_core(table):
    half = NF // 2
    low, high = table[:half].reshape(NF, NT), table[half:].reshape(NF, NT)
    return np.stack([np.concatenate([low, high]), np.concatenate([high, low])])


def parts(table):
    high = table.astype(ml_dtypes.bfloat16)
    low = (table - high.astype(np.float64)).astype(ml_dtypes.bfloat16)
    return high, low


def split(x):
    high = x.astype(BF16)
    return high, (x - high.astype(F32)).astype(BF16)


def bins_of(half):
    return tuple(half * share // sum(SHARES) for share in SHARES)


def forward_kernel(counts, core_ref, w_ref, x_ref, *out_refs):
    rows, m, t = x_ref.shape
    group = 8

    def some(q, carry):
        first = pl.multiple_of(q * group, group)
        high, low = split(x_ref[pl.ds(first, group)].reshape(group * m, t))
        x = jnp.concatenate([high, low], axis=1)
        both = lax.dot_general(w_ref[0], x, (((1,), (1,)), ((), ())), preferred_element_type=F32)
        n = both.shape[0] // 2
        res = both[:n] + both[n:]
        at = 0
        for out, count in zip(out_refs, counts):
            view = out.at[:, pl.ds(first, group), :]
            for i in range(group):
                view[:, i, :] = res[at : at + count, i * m : (i + 1) * m]
            at += count
        return carry

    lax.fori_loop(0, rows // group, some, 0)


def forward(x, core, cuts, start=0, n=None):
    m, t = x.shape[1:]
    n = x.shape[0] if n is None else n
    table = by_core(tables()[0])
    table = np.concatenate([table[:, a:b] for a, b in cuts], axis=1)
    counts = [b - a for a, b in cuts]
    shapes = [jax.ShapeDtypeStruct((count, n, m), F32) for count in counts]
    high, low = parts(table)
    w = np.concatenate(
        [np.concatenate([high, high], axis=2), np.concatenate([low, np.zeros_like(low)], axis=2)], axis=1
    )
    step = 32 if n > 64 else 16
    return pl.pallas_call(
        functools.partial(forward_kernel, counts),
        grid_spec=pltpu.PrefetchScalarGridSpec(
            num_scalar_prefetch=1,
            grid=(n // step,),
            in_specs=[
                pl.BlockSpec((1,) + w.shape[1:], lambda i, c: (c[0], 0, 0)),
                pl.BlockSpec((step, m, t), lambda i, c: (i + start // step, 0, 0)),
            ],
            out_specs=[pl.BlockSpec((s.shape[0], step, m), lambda i, c: (0, i, 0)) for s in shapes],
        ),
        out_shape=shapes,
        cost_estimate=pl.CostEstimate(
            flops=12 * n * m * t * NT, bytes_accessed=8 * n * m * t, transcendentals=0
        ),
        name="forward",
    )(core, jnp.asarray(w), x)


ALL, EARLY, LATE = range(3)


def sides(part, levels):
    pairs = [[("own", 0)]] + [[("up", s), ("down", levels - s)] for s in range(1, levels)]
    return [[x for x in pair if part != EARLY or x[1] < levels - 1] for pair in pairs]


def product_kernel(part, levels, places, d_keys, g_keys, slot_ref, *refs):
    d_refs = {}
    for (a, at), ref in zip(d_keys, refs):
        d_refs.setdefault(a, []).append((at, ref))
    g_refs = {}
    for (way, hop, h), ref in zip(g_keys, refs[len(d_keys) :]):
        for i in range(2) if h is None else (h,):
            g_refs[way, hop, i] = ref.at[i] if h is None else ref
    rest = refs[len(d_keys) + len(g_keys) :]
    lhs, rhs = rest[-2:]
    count = refs[0].shape[0] // 2
    depth = refs[0].shape[2]
    rows = lhs.shape[1] // 4
    half, cols = next(iter(g_refs.values())).shape[1:]
    core, chosen, far = (slot_ref[levels + i] for i in range(3))
    step, each = pl.program_id(0), 4 // count

    def put_g(b, slot, h, half_of, g):
        high, low = split(g)
        place = jnp.where(core == h, 0, half)
        at = pl.multiple_of(slot * 3 * depth + place, half)
        to = slice(half_of * cols, (half_of + 1) * cols)
        for i, value in enumerate((high, high, low)):
            rhs[b % 2, pl.ds(at + i * depth, half), to] = value

    def put_d(b, place, which):
        for i, (at, ref) in enumerate(d_refs[which[0]]):
            for half_of in range(2):
                value = ref[2 * b + half_of]
                for a in which[1:]:
                    value = jnp.where(chosen == a, d_refs[a][i][1][2 * b + half_of], value)
                high, low = split(value)
                first = 2 * rows * half_of + at
                for j, piece in enumerate((high, low, high)):
                    to = slice((3 * place + j) * depth, (3 * place + j + 1) * depth)
                    lhs[b % 2, first : first + ref.shape[1], to] = piece

    for b in range(count):
        for h in range(2):
            for half_of in range(2):
                row = 2 * b + half_of
                blocks = [sum(g_refs[way, hop, h][row] for way, hop in pair) for pair in sides(part, levels)]
                if part == LATE:
                    met = blocks[0]
                    for s in range(1, levels):
                        met = jnp.where(slot_ref[s] == 0, blocks[s], met)
                    last = g_refs["up", levels - 1, h][row] + g_refs["down", levels - 1, h][row]
                    put_g(b, 0, h, half_of, met)
                    put_g(b, 1, h, half_of, jnp.where(far > 0, last, 0.0))
                else:
                    for s, block in enumerate(blocks):
                        put_g(b, slot_ref[s], h, half_of, block)
        for place, which in enumerate(places):
            put_d(b, place, which)
        deep = 3 * depth * len(places)
        p = jnp.dot(lhs[b % 2, :, :deep], rhs[b % 2, :deep, :], preferred_element_type=F32)
        real = p[: 2 * rows, :cols] - p[2 * rows :, cols:]
        imaginary = p[: 2 * rows, cols:] + p[2 * rows :, :cols]
        if part == EARLY:
            rest[0][2 * b], rest[0][2 * b + 1] = real, imaginary
            continue
        if part == LATE:
            real, imaginary = real + rest[0][2 * b], imaginary + rest[0][2 * b + 1]
        held = rest[-3]
        row = 2 * (step % each * count + b)
        held[row], held[row + 1] = real, imaginary

    if part != EARLY:

        @pl.when(step % each == each - 1)
        def _():
            out_a, out_b, held = rest[-5:-2]
            for c in range(held.shape[0]):
                out_a[:, c, :] = held[c, :rows]
                out_b[:, c, :] = held[c, rows:]


def numbers(part, me, d, g):
    slot, core, z = me
    levels = slot.shape[0]
    around = len(d)
    diag = around // 2
    far_a = slot[jnp.where(z == 0, 1, levels - 1)]
    far = ((z == 0) | (z == levels - 1)) & (far_a != diag)
    chosen = jnp.where(far, far_a, 0)
    others = [a for a in range(around) if a != diag]
    if part == ALL:
        places, to = [[a] for a in range(around)], slot
    elif part == EARLY:
        places, to = [[a] for a in others], jnp.where(slot == diag, len(others), slot - (slot > diag))
    else:
        places, to = [[diag], others], jnp.where(slot == diag, 0, 2)
    needed = []
    for a in sorted(set(sum(places, []))):
        needed += [chosen == a if part == LATE and a != diag else True] * d[a]
    for s, pair in enumerate(sides(part, levels)):
        for way, hop in pair:
            there = {"own": True, "up": z >= hop, "down": z + hop < levels}[way]
            if part == LATE:
                there = there & ((slot[s] == diag) | (hop == levels - 1))
            needed += [there] * g
    needed.append(True)
    scalars = [core, chosen, far] + needed
    scalars = [to.astype(jnp.int32), jnp.stack([jnp.asarray(x).astype(jnp.int32) for x in scalars])]
    return places, jnp.concatenate(scalars)


def product(part, places, scalars, d, g, so_far=None):
    levels = 1 + max(hop for _, hop in g)
    depth = d[0][0].shape[2]
    n = d[0][0].shape[0]
    rows = sum(x.shape[1] for x in d[0]) // 2
    _, cols = g["own", 0][0].shape[-2:]
    step = 4
    operands, d_keys, g_keys = [], [], []
    for a in sorted(set(sum(places, []))):
        at = 0
        for x in d[a]:
            d_keys.append((a, at))
            operands.append(x)
            at += x.shape[1]
    for pair in sides(part, levels):
        for way, hop in pair:
            for h, x in enumerate(g[way, hop]):
                g_keys.append((way, hop, h if len(g[way, hop]) == 2 else None))
                operands.append(x)
    small = 8 * n * rows * cols <= SMALL
    if so_far is not None:
        operands.append(pltpu.with_memory_space_constraint(so_far, pltpu.VMEM) if small else so_far)
    first = levels + 3

    def spec(i, x):
        at = lambda j, c: jnp.where(c[first + i] > 0, j, 0)
        if x.ndim == 4:
            return pl.BlockSpec((2, step) + x.shape[2:], lambda j, c: (0, at(j, c), 0, 0))
        return pl.BlockSpec((step,) + x.shape[1:], lambda j, c: (at(j, c), 0, 0))

    scratch = [
        pltpu.VMEM((2, 4 * rows, 3 * depth * len(places)), BF16),
        pltpu.VMEM((2, 3 * depth * (len(places) + 1), 2 * cols), BF16),
    ]
    if part == EARLY:
        out = (pltpu.VMEM if small else jax.ShapeDtypeStruct)((n, 2 * rows, cols), F32)
        out_specs = pl.BlockSpec((step, 2 * rows, cols), lambda i, c: (i, 0, 0))
    else:
        out = [jax.ShapeDtypeStruct((rows, n, cols), F32)] * 2
        out_specs = [pl.BlockSpec((rows, 8, cols), lambda i, c: (0, i * step // 8, 0))] * 2
        scratch = [pltpu.VMEM((8, 2 * rows, cols), F32)] + scratch
    return pl.pallas_call(
        functools.partial(product_kernel, part, levels, places, d_keys, g_keys),
        grid_spec=pltpu.PrefetchScalarGridSpec(
            num_scalar_prefetch=1,
            grid=(n // step,),
            in_specs=[spec(i, x) for i, x in enumerate(operands)],
            out_specs=out_specs,
            scratch_shapes=scratch,
        ),
        out_shape=out,
        compiler_params=pltpu.CompilerParams(vmem_limit_bytes=GRANT if part == LATE and small else None),
        cost_estimate=pl.CostEstimate(
            flops=n // 2 * 2 * 4 * rows * 3 * len(places) * depth * 2 * cols,
            bytes_accessed=4 * sum(x.size for x in operands),
            transcendentals=0,
        ),
    )(scalars, *operands)


def inverse_kernel(count, core_ref, w_ref, *refs):
    x_refs, out = refs[:count], refs[-1]
    group = 8

    def some(q, carry):
        for u in range(group):
            i = q * group + u
            high, low = split(jnp.concatenate([x[i] for x in x_refs], axis=0))
            x = jnp.concatenate([high, low], axis=0)
            both = lax.dot_general(x, w_ref[0], (((0,), (0,)), ((), ())), preferred_element_type=F32)
            res = both[:, :NT] + both[:, NT:]
            out[i] = res if len(refs) == count + 1 else res + refs[count][i]
        return carry

    lax.fori_loop(0, out.shape[0] // group, some, 0)


def inverse(ms, core, cuts, so_far=None):
    rows, _, cols = ms[0].shape
    table = by_core(tables()[1])
    high, low = parts(np.concatenate([table[:, a:b] for a, b in cuts], axis=1))
    operands = list(ms) + ([] if so_far is None else [pltpu.with_memory_space_constraint(so_far, pltpu.VMEM)])
    w = np.concatenate(
        [np.concatenate([high, low], axis=2), np.concatenate([high, np.zeros_like(low)], axis=2)], axis=1
    )
    step = 32
    return pl.pallas_call(
        functools.partial(inverse_kernel, len(ms)),
        grid_spec=pltpu.PrefetchScalarGridSpec(
            num_scalar_prefetch=1,
            grid=(rows // step,),
            in_specs=[pl.BlockSpec((1,) + w.shape[1:], lambda i, c: (c[0], 0, 0))]
            + [pl.BlockSpec((step,) + x.shape[1:], lambda i, c: (i, 0, 0)) for x in operands],
            out_specs=pl.BlockSpec((step, cols, NT), lambda i, c: (i, 0, 0)),
        ),
        out_shape=(pltpu.VMEM if so_far is None else jax.ShapeDtypeStruct)((rows, cols, NT), F32),
        compiler_params=pltpu.CompilerParams(vmem_limit_bytes=GRANT - (8 << 20)),
        cost_estimate=pl.CostEstimate(
            flops=12 * rows * cols * NT * NT, bytes_accessed=8 * rows * cols * NT, transcendentals=0
        ),
        name="inverse",
    )(core, jnp.asarray(w), *operands)


def plain(recorded, panels):
    forth, back = (jnp.asarray(x, F32) for x in tables())
    best = lax.Precision.HIGHEST
    to_bins = lambda x: lax.all_to_all(
        jnp.einsum("fct,abt->fcab", forth, x, precision=best), "freq", split_axis=0, concat_axis=3, tiled=True
    )
    d = to_bins(recorded)
    g = lax.all_gather(to_bins(panels), "src", axis=2, tiled=True)
    mul = functools.partial(jnp.einsum, "fik,fkr->fir", precision=best)
    re = mul(d[:, 0], g[:, 0]) - mul(d[:, 1], g[:, 1])
    im = mul(d[:, 0], g[:, 1]) + mul(d[:, 1], g[:, 0])
    m = lax.all_to_all(jnp.stack([re, im], axis=1), "freq", split_axis=3, concat_axis=0, tiled=True)
    return jnp.einsum("fcir,fct->irt", m, back, precision=best)


def local(around, along, recorded, panels):
    tiled = all(x.shape[1] % 128 == 0 and x.shape[0] % 32 == 0 for x in (recorded, panels))
    if around != 4 or along != 8 or not tiled:
        return plain(recorded, panels)
    half = NF // 2
    levels = along // 2
    ring = list(range(around // 2)) + list(range(around - 1, around // 2 - 1, -1))
    clockwise = [(ring[i], ring[(i + 1) % around]) for i in range(around)]
    counter = [(b, a) for a, b in clockwise]
    upward = [(2 * z + c, 2 * z + 2 + c) for z in range(levels - 1) for c in range(2)]
    downward = [(b, a) for a, b in upward]
    partner = [(i, i ^ 1) for i in range(along)]

    me_ring, me_src = lax.axis_index("freq"), lax.axis_index("src")
    core, z = me_src % 2, me_src // 2
    at = jnp.where(me_ring < around // 2, me_ring, around // 2 + around - 1 - me_ring)
    core_at = core.astype(jnp.int32).reshape(1)
    bins = bins_of(half)
    chunks = len(bins)
    where = jnp.asarray(np.argsort(ring), jnp.int32)
    slot = ((at - where[(z - jnp.arange(levels)) % levels]) % around).astype(jnp.int32)
    me = (slot, core.astype(jnp.int32), z)
    edges = [int(e) for e in np.cumsum([0] + [2 * b for b in bins])]
    cuts = list(zip(edges[:-1], edges[1:]))
    cuts += [(NF + a, NF + b) for a, b in cuts]

    def transform(*args):
        return list(forward(*args))

    n = recorded.shape[0]
    ahead = n // 4
    head = transform(recorded, core_at, cuts[:1], 0, ahead)
    g_parts = transform(panels, core_at, cuts[:1])
    d_parts = transform(recorded, core_at, cuts[:1], ahead, n - ahead)
    g_parts += transform(panels, core_at, cuts[1:])
    d_parts += transform(recorded, core_at, cuts[1:])
    ms = []
    for c in range(chunks):
        g_own = [g_parts[c], lax.ppermute(g_parts[chunks + c], "src", partner)]
        d_swapped = lax.ppermute(d_parts[chunks + c], "src", partner)
        d_own = [d_parts[c], d_swapped] if c else head + [d_parts[c], d_swapped]
        calls = (EARLY, LATE) if c in SPLIT else (ALL,)
        counts = {a: len(d_own) for a in range(around)}
        plans = [numbers(part, me, counts, 2) for part in calls]
        g = {("own", 0): g_own}
        up, down = g_own, g_own
        for s in range(1, levels):
            if s == 2:
                made, up[0] = lax.optimization_barrier(([x[1] for x in plans], up[0]))
                plans = [(x[0], y) for x, y in zip(plans, made)]
            up = [lax.ppermute(x, "src", upward) for x in up]
            down = [lax.ppermute(x, "src", downward) for x in down]
            g["up", s], g["down", s] = up, down
        d = {0: d_own}
        right, left = d_own, d_own
        for a in range(1, around // 2):
            right = [lax.ppermute(x, "freq", clockwise) for x in right]
            left = [lax.ppermute(x, "freq", counter) for x in left]
            d[a], d[around - a] = right, left
        last = around // 2
        mine = len(d_own) - 1
        d[last] = [lax.ppermute(x, "freq", clockwise) for x in right[:mine]]
        d[last].append(lax.ppermute(left[mine], "freq", counter))
        m = None
        for part, (places, scalars) in zip(calls, plans):
            m = product(part, places, scalars, d, g, m)
        ms.append([m[0], lax.ppermute(m[1], "src", partner)])
    acc = inverse(ms[0], core_at, [cuts[0], cuts[chunks]])
    return inverse(ms[1], core_at, [cuts[1], cuts[chunks + 1]], acc)


def solution(mesh):
    return jax.shard_map(
        functools.partial(local, mesh.shape["freq"], mesh.shape["src"]),
        mesh=mesh,
        in_specs=(P("src", "freq", None), P("src", "freq", None)),
        out_specs=P("src", "freq", None),
        check_vma=False,
    )
```

```python
import functools

import jax
import jax.numpy as jnp
import ml_dtypes
import numpy as np
from jax import lax
from jax.experimental import pallas as pl
from jax.experimental.pallas import tpu as pltpu
from jax.sharding import PartitionSpec as P


NT = 128
NF = 64
SPLIT = (0, 1)
SHARES = (20, 12)
SMALL = 4 << 20
GRANT = 46 << 20
F32, BF16 = jnp.float32, jnp.bfloat16


def tables():
    phase = np.arange(NF)[:, None] * np.arange(NT)[None, :] % NT
    angle = 2.0 * np.pi / NT * phase
    forward = np.stack([np.cos(angle), -np.sin(angle)], axis=1)
    weight = np.where(np.arange(NF) == 0, 1.0, 2.0) / NT
    return forward, forward * weight[:, None, None]


def by_core(table):
    half = NF // 2
    low, high = table[:half].reshape(NF, NT), table[half:].reshape(NF, NT)
    return np.stack([np.concatenate([low, high]), np.concatenate([high, low])])


def parts(table):
    high = table.astype(ml_dtypes.bfloat16)
    low = (table - high.astype(np.float64)).astype(ml_dtypes.bfloat16)
    return high, low


def split(x):
    high = x.astype(BF16)
    return high, (x - high.astype(F32)).astype(BF16)


def bins_of(half):
    return tuple(half * share // sum(SHARES) for share in SHARES)


def forward_kernel(counts, core_ref, w_ref, x_ref, *out_refs):
    rows, m, t = x_ref.shape
    group = 8

    def some(q, carry):
        first = pl.multiple_of(q * group, group)
        high, low = split(x_ref[pl.ds(first, group)].reshape(group * m, t))
        x = jnp.concatenate([high, low], axis=1)
        both = lax.dot_general(w_ref[0], x, (((1,), (1,)), ((), ())), preferred_element_type=F32)
        n = both.shape[0] // 2
        res = both[:n] + both[n:]
        at = 0
        for out, count in zip(out_refs, counts):
            view = out.at[:, pl.ds(first, group), :]
            for r in range(0, count, group):
                eight = [res[at + r : at + r + group, i * m : (i + 1) * m] for i in range(group)]
                view[r : r + group] = jnp.swapaxes(jnp.stack(eight), 0, 1)
            at += count
        return carry

    lax.fori_loop(0, rows // group, some, 0)


def forward(x, core, cuts, start=0, n=None):
    m, t = x.shape[1:]
    n = x.shape[0] if n is None else n
    table = by_core(tables()[0])
    table = np.concatenate([table[:, a:b] for a, b in cuts], axis=1)
    counts = [b - a for a, b in cuts]
    shapes = [jax.ShapeDtypeStruct((count, n, m), F32) for count in counts]
    high, low = parts(table)
    w = np.concatenate(
        [np.concatenate([high, high], axis=2), np.concatenate([low, np.zeros_like(low)], axis=2)], axis=1
    )
    step = 32 if n >= 64 else 16
    return pl.pallas_call(
        functools.partial(forward_kernel, counts),
        grid_spec=pltpu.PrefetchScalarGridSpec(
            num_scalar_prefetch=1,
            grid=(n // step,),
            in_specs=[
                pl.BlockSpec((1,) + w.shape[1:], lambda i, c: (c[0], 0, 0)),
                pl.BlockSpec((step, m, t), lambda i, c: (i + start // step, 0, 0)),
            ],
            out_specs=[pl.BlockSpec((s.shape[0], step, m), lambda i, c: (0, i, 0)) for s in shapes],
        ),
        out_shape=shapes,
        cost_estimate=pl.CostEstimate(
            flops=12 * n * m * t * NT, bytes_accessed=8 * n * m * t, transcendentals=0
        ),
        name="forward",
    )(core, jnp.asarray(w), x)


ALL, EARLY, LATE = range(3)


def sides(part, levels):
    pairs = [[("own", 0)]] + [[("up", s), ("down", levels - s)] for s in range(1, levels)]
    return [[x for x in pair if part != EARLY or x[1] < levels - 1] for pair in pairs]


def product_kernel(part, levels, places, d_keys, g_keys, slot_ref, *refs):
    d_refs = {}
    for (a, at), ref in zip(d_keys, refs):
        d_refs.setdefault(a, []).append((at, ref))
    g_refs = {}
    for (way, hop, h), ref in zip(g_keys, refs[len(d_keys) :]):
        for i in range(2) if h is None else (h,):
            g_refs[way, hop, i] = ref.at[i] if h is None else ref
    rest = refs[len(d_keys) + len(g_keys) :]
    lhs, rhs = rest[-2:]
    count = refs[0].shape[0] // 2
    depth = refs[0].shape[2]
    rows = lhs.shape[1] // 4
    half, cols = next(iter(g_refs.values())).shape[1:]
    core, chosen, far = (slot_ref[levels + i] for i in range(3))
    step, each = pl.program_id(0), 4 // count

    def put_g(b, slot, h, half_of, g):
        high, low = split(g)
        place = jnp.where(core == h, 0, half)
        at = pl.multiple_of(slot * 3 * depth + place, half)
        to = slice(half_of * cols, (half_of + 1) * cols)
        for i, value in enumerate((high, high, low)):
            rhs[b % 2, pl.ds(at + i * depth, half), to] = value

    def put_d(b, place, which):
        for i, (at, ref) in enumerate(d_refs[which[0]]):
            for half_of in range(2):
                value = ref[2 * b + half_of]
                for a in which[1:]:
                    value = jnp.where(chosen == a, d_refs[a][i][1][2 * b + half_of], value)
                high, low = split(value)
                first = 2 * rows * half_of + at
                for j, piece in enumerate((high, low, high)):
                    to = slice((3 * place + j) * depth, (3 * place + j + 1) * depth)
                    lhs[b % 2, first : first + ref.shape[1], to] = piece

    for b in range(count):
        for h in range(2):
            for half_of in range(2):
                row = 2 * b + half_of
                blocks = [sum(g_refs[way, hop, h][row] for way, hop in pair) for pair in sides(part, levels)]
                if part == LATE:
                    met = blocks[0]
                    for s in range(1, levels):
                        met = jnp.where(slot_ref[s] == 0, blocks[s], met)
                    last = g_refs["up", levels - 1, h][row] + g_refs["down", levels - 1, h][row]
                    put_g(b, 0, h, half_of, met)
                    put_g(b, 1, h, half_of, jnp.where(far > 0, last, 0.0))
                else:
                    for s, block in enumerate(blocks):
                        put_g(b, slot_ref[s], h, half_of, block)
        for place, which in enumerate(places):
            put_d(b, place, which)
        deep = 3 * depth * len(places)
        p = jnp.dot(lhs[b % 2, :, :deep], rhs[b % 2, :deep, :], preferred_element_type=F32)
        real = p[: 2 * rows, :cols] - p[2 * rows :, cols:]
        imaginary = p[: 2 * rows, cols:] + p[2 * rows :, :cols]
        if part == EARLY:
            rest[0][2 * b], rest[0][2 * b + 1] = real, imaginary
            continue
        if part == LATE:
            real, imaginary = real + rest[0][2 * b], imaginary + rest[0][2 * b + 1]
        held = rest[-3]
        row = 2 * (step % each * count + b)
        held[row], held[row + 1] = real, imaginary

    if part != EARLY:

        @pl.when(step % each == each - 1)
        def _():
            out_a, out_b, held = rest[-5:-2]
            for i in range(0, rows, 8):
                out_a[i : i + 8] = jnp.swapaxes(held[:, i : i + 8, :], 0, 1)
                out_b[i : i + 8] = jnp.swapaxes(held[:, rows + i : rows + i + 8, :], 0, 1)


def numbers(part, me, d, g):
    slot, core, z = me
    levels = slot.shape[0]
    around = len(d)
    diag = around // 2
    far_a = slot[jnp.where(z == 0, 1, levels - 1)]
    far = ((z == 0) | (z == levels - 1)) & (far_a != diag)
    chosen = jnp.where(far, far_a, 0)
    others = [a for a in range(around) if a != diag]
    if part == ALL:
        places, to = [[a] for a in range(around)], slot
    elif part == EARLY:
        places, to = [[a] for a in others], jnp.where(slot == diag, len(others), slot - (slot > diag))
    else:
        places, to = [[diag], others], jnp.where(slot == diag, 0, 2)
    needed = []
    for a in sorted(set(sum(places, []))):
        needed += [chosen == a if part == LATE and a != diag else True] * d[a]
    for s, pair in enumerate(sides(part, levels)):
        for way, hop in pair:
            there = {"own": True, "up": z >= hop, "down": z + hop < levels}[way]
            if part == LATE:
                there = there & ((slot[s] == diag) | (hop == levels - 1))
            needed += [there] * g
    needed.append(True)
    scalars = [core, chosen, far] + needed
    scalars = [to.astype(jnp.int32), jnp.stack([jnp.asarray(x).astype(jnp.int32) for x in scalars])]
    return places, jnp.concatenate(scalars)


def product(part, places, scalars, d, g, so_far=None):
    levels = 1 + max(hop for _, hop in g)
    depth = d[0][0].shape[2]
    n = d[0][0].shape[0]
    rows = sum(x.shape[1] for x in d[0]) // 2
    _, cols = g["own", 0][0].shape[-2:]
    step = 4
    operands, d_keys, g_keys = [], [], []
    for a in sorted(set(sum(places, []))):
        at = 0
        for x in d[a]:
            d_keys.append((a, at))
            operands.append(x)
            at += x.shape[1]
    for pair in sides(part, levels):
        for way, hop in pair:
            for h, x in enumerate(g[way, hop]):
                g_keys.append((way, hop, h if len(g[way, hop]) == 2 else None))
                operands.append(x)
    small = 8 * n * rows * cols <= SMALL
    if so_far is not None:
        operands.append(pltpu.with_memory_space_constraint(so_far, pltpu.VMEM) if small else so_far)
    first = levels + 3

    def spec(i, x):
        at = lambda j, c: jnp.where(c[first + i] > 0, j, 0)
        if x.ndim == 4:
            return pl.BlockSpec((2, step) + x.shape[2:], lambda j, c: (0, at(j, c), 0, 0))
        return pl.BlockSpec((step,) + x.shape[1:], lambda j, c: (at(j, c), 0, 0))

    scratch = [
        pltpu.VMEM((2, 4 * rows, 3 * depth * len(places)), BF16),
        pltpu.VMEM((2, 3 * depth * (len(places) + 1), 2 * cols), BF16),
    ]
    if part == EARLY:
        out = (pltpu.VMEM if small else jax.ShapeDtypeStruct)((n, 2 * rows, cols), F32)
        out_specs = pl.BlockSpec((step, 2 * rows, cols), lambda i, c: (i, 0, 0))
    else:
        out = [jax.ShapeDtypeStruct((rows, n, cols), F32)] * 2
        out_specs = [pl.BlockSpec((rows, 8, cols), lambda i, c: (0, i * step // 8, 0))] * 2
        scratch = [pltpu.VMEM((8, 2 * rows, cols), F32)] + scratch
    return pl.pallas_call(
        functools.partial(product_kernel, part, levels, places, d_keys, g_keys),
        grid_spec=pltpu.PrefetchScalarGridSpec(
            num_scalar_prefetch=1,
            grid=(n // step,),
            in_specs=[spec(i, x) for i, x in enumerate(operands)],
            out_specs=out_specs,
            scratch_shapes=scratch,
        ),
        out_shape=out,
        compiler_params=pltpu.CompilerParams(vmem_limit_bytes=GRANT if part == LATE and small else None),
        cost_estimate=pl.CostEstimate(
            flops=n // 2 * 2 * 4 * rows * 3 * len(places) * depth * 2 * cols,
            bytes_accessed=4 * sum(x.size for x in operands),
            transcendentals=0,
        ),
    )(scalars, *operands)


def inverse_kernel(count, core_ref, w_ref, *refs):
    x_refs, out = refs[:count], refs[-1]
    group = 8

    def some(q, carry):
        for u in range(group):
            i = q * group + u
            high, low = split(jnp.concatenate([x[i] for x in x_refs], axis=0))
            x = jnp.concatenate([high, low], axis=0)
            both = lax.dot_general(x, w_ref[0], (((0,), (0,)), ((), ())), preferred_element_type=F32)
            res = both[:, :NT] + both[:, NT:]
            out[i] = res if len(refs) == count + 1 else res + refs[count][i]
        return carry

    lax.fori_loop(0, out.shape[0] // group, some, 0)


def inverse(ms, core, cuts, so_far=None):
    rows, _, cols = ms[0].shape
    table = by_core(tables()[1])
    high, low = parts(np.concatenate([table[:, a:b] for a, b in cuts], axis=1))
    operands = list(ms) + ([] if so_far is None else [pltpu.with_memory_space_constraint(so_far, pltpu.VMEM)])
    w = np.concatenate(
        [np.concatenate([high, low], axis=2), np.concatenate([high, np.zeros_like(low)], axis=2)], axis=1
    )
    step = 32
    return pl.pallas_call(
        functools.partial(inverse_kernel, len(ms)),
        grid_spec=pltpu.PrefetchScalarGridSpec(
            num_scalar_prefetch=1,
            grid=(rows // step,),
            in_specs=[pl.BlockSpec((1,) + w.shape[1:], lambda i, c: (c[0], 0, 0))]
            + [pl.BlockSpec((step,) + x.shape[1:], lambda i, c: (i, 0, 0)) for x in operands],
            out_specs=pl.BlockSpec((step, cols, NT), lambda i, c: (i, 0, 0)),
        ),
        out_shape=(pltpu.VMEM if so_far is None else jax.ShapeDtypeStruct)((rows, cols, NT), F32),
        compiler_params=pltpu.CompilerParams(vmem_limit_bytes=GRANT - (8 << 20)),
        cost_estimate=pl.CostEstimate(
            flops=12 * rows * cols * NT * NT, bytes_accessed=8 * rows * cols * NT, transcendentals=0
        ),
        name="inverse",
    )(core, jnp.asarray(w), *operands)


def plain(recorded, panels):
    forth, back = (jnp.asarray(x, F32) for x in tables())
    best = lax.Precision.HIGHEST
    to_bins = lambda x: lax.all_to_all(
        jnp.einsum("fct,abt->fcab", forth, x, precision=best), "freq", split_axis=0, concat_axis=3, tiled=True
    )
    d = to_bins(recorded)
    g = lax.all_gather(to_bins(panels), "src", axis=2, tiled=True)
    mul = functools.partial(jnp.einsum, "fik,fkr->fir", precision=best)
    re = mul(d[:, 0], g[:, 0]) - mul(d[:, 1], g[:, 1])
    im = mul(d[:, 0], g[:, 1]) + mul(d[:, 1], g[:, 0])
    m = lax.all_to_all(jnp.stack([re, im], axis=1), "freq", split_axis=3, concat_axis=0, tiled=True)
    return jnp.einsum("fcir,fct->irt", m, back, precision=best)


def local(around, along, recorded, panels):
    tiled = all(x.shape[1] % 128 == 0 and x.shape[0] % 32 == 0 for x in (recorded, panels))
    if around != 4 or along != 8 or not tiled:
        return plain(recorded, panels)
    half = NF // 2
    levels = along // 2
    ring = list(range(around // 2)) + list(range(around - 1, around // 2 - 1, -1))
    clockwise = [(ring[i], ring[(i + 1) % around]) for i in range(around)]
    counter = [(b, a) for a, b in clockwise]
    upward = [(2 * z + c, 2 * z + 2 + c) for z in range(levels - 1) for c in range(2)]
    downward = [(b, a) for a, b in upward]
    partner = [(i, i ^ 1) for i in range(along)]

    me_ring, me_src = lax.axis_index("freq"), lax.axis_index("src")
    core, z = me_src % 2, me_src // 2
    at = jnp.where(me_ring < around // 2, me_ring, around // 2 + around - 1 - me_ring)
    core_at = core.astype(jnp.int32).reshape(1)
    bins = bins_of(half)
    chunks = len(bins)
    where = jnp.asarray(np.argsort(ring), jnp.int32)
    slot = ((at - where[(z - jnp.arange(levels)) % levels]) % around).astype(jnp.int32)
    me = (slot, core.astype(jnp.int32), z)
    edges = [int(e) for e in np.cumsum([0] + [2 * b for b in bins])]
    cuts = list(zip(edges[:-1], edges[1:]))
    cuts += [(NF + a, NF + b) for a, b in cuts]

    def transform(*args):
        return list(forward(*args))

    n = recorded.shape[0]
    ahead = n // 4
    head = transform(recorded, core_at, cuts[:1], 0, ahead)
    g_parts = transform(panels, core_at, cuts[:1])
    d_parts = transform(recorded, core_at, cuts[:1], ahead, n - ahead)
    g_parts += transform(panels, core_at, cuts[1:])
    d_parts += transform(recorded, core_at, cuts[1:])
    ms = []
    for c in range(chunks):
        g_own = [g_parts[c], lax.ppermute(g_parts[chunks + c], "src", partner)]
        d_swapped = lax.ppermute(d_parts[chunks + c], "src", partner)
        d_own = [d_parts[c], d_swapped] if c else head + [d_parts[c], d_swapped]
        calls = (EARLY, LATE) if c in SPLIT else (ALL,)
        counts = {a: len(d_own) for a in range(around)}
        plans = [numbers(part, me, counts, 1 if c else 2) for part in calls]
        if c:
            g_own = [jnp.stack(g_own)]
        g = {("own", 0): g_own}
        up, down = g_own, g_own
        for s in range(1, levels):
            if s == 2:
                made, up[0] = lax.optimization_barrier(([x[1] for x in plans], up[0]))
                plans = [(x[0], y) for x, y in zip(plans, made)]
            up = [lax.ppermute(x, "src", upward) for x in up]
            down = [lax.ppermute(x, "src", downward) for x in down]
            g["up", s], g["down", s] = up, down
        d = {0: d_own}
        right, left = d_own, d_own
        for a in range(1, around // 2):
            right = [lax.ppermute(x, "freq", clockwise) for x in right]
            left = [lax.ppermute(x, "freq", counter) for x in left]
            d[a], d[around - a] = right, left
        last = around // 2
        mine = len(d_own) - 1
        d[last] = [lax.ppermute(x, "freq", clockwise) for x in right[:mine]]
        d[last].append(lax.ppermute(left[mine], "freq", counter))
        m = None
        for part, (places, scalars) in zip(calls, plans):
            m = product(part, places, scalars, d, g, m)
        ms.append([m[0], lax.ppermute(m[1], "src", partner)])
    acc = inverse(ms[0], core_at, [cuts[0], cuts[chunks]])
    return inverse(ms[1], core_at, [cuts[1], cuts[chunks + 1]], acc)


def solution(mesh):
    return jax.shard_map(
        functools.partial(local, mesh.shape["freq"], mesh.shape["src"]),
        mesh=mesh,
        in_specs=(P("src", "freq", None), P("src", "freq", None)),
        out_specs=P("src", "freq", None),
        check_vma=False,
    )
```
